256 devices in a mesh: gx: 8 (over y, core), gy: 4 (over z_lo), gz: 8 (over x, z_hi).
Axes of the slice: x: 4, y: 4, z: 8 (z_hi: 2, z_lo: 4; z = z_hi * 4 + z_lo), core: 2. Of those that a mesh axis runs over, the one named last changes fastest.
Arguments:
- wavefunctions: float32 [96, 48, 96, 256], P('gx', 'gy', 'gz'), may hold values from -6 to 6
- cell_matrices: bfloat16 [16, 8, 16, 343, 343], P('gx', 'gy', 'gz'), may hold values from -0.078125 to 0.078125
- projectors: float32 [256, 16, 1728], P(('gx', 'gy', 'gz')), may hold values from -0.14433756 to 0.14433756
- slot_atoms: int32 [256, 16], P(('gx', 'gy', 'gz')), may hold values from 0 to 512, as said below
- atom_coupling: float32 [512], replicated, may hold values from 0.5 to 3
Outputs:
- filtered: float32 [96, 48, 96, 256], P('gx', 'gy', 'gz')
The draws below stay inside these ranges and needn't reach their ends.
Inputs may be any that keep to these rules, and one draw needn't show every extreme that they name: `slot_atoms`: atom a belongs to device a // 2. The live slots of device d name distinct atoms whose owners lie 0 or 1 below d along each of gx, gy, gz (periodically); 512 marks an empty slot, and some device has all 16 slots live.
All inputs are finite; a program needn't handle non-finite values.
Results may differ from the reference program's by a relative error of at most 0.00045.
Values may be sent and summed in bfloat16 or wider, within the bound.
A program may use at most 64 MiB of HBM per device.

```python
import jax
import jax.numpy as jnp
from jax import lax

CELL_NODES = 343
WAVES = 256
DEGREE = 2
ATOM_DEV = 2
SLOTS = 16
NATOMS = 512
NODES_DEV = 1728
NNX = 96
NNY = 48
NNZ = 96
NCX = 16
NCY = 8
NCZ = 16
N_GX = 8
N_GY = 4
N_GZ = 8
DEVICES = 256


def draw_slot_atoms(key, part):
    candidates = 8 * ATOM_DEV
    device_keys = jax.random.split(jax.random.fold_in(key, 11), DEVICES)
    orders = jax.vmap(lambda one_key: jax.random.permutation(one_key, candidates))(device_keys)
    live_count = jax.random.randint(jax.random.fold_in(key, 12), (DEVICES,), 1, SLOTS // 4 + 2)
    busy_pick = jax.random.randint(jax.random.fold_in(key, 13), (DEVICES,), 0, 16)
    full_device = jax.random.randint(jax.random.fold_in(key, 14), (), 0, DEVICES)
    device_ids = jnp.arange(DEVICES)
    live_count = jnp.where((busy_pick == 0) | (device_ids == full_device), SLOTS, live_count)
    live_count = jnp.minimum(live_count, SLOTS)
    index_x = device_ids // (N_GY * N_GZ)
    index_y = device_ids // N_GZ % N_GY
    index_z = device_ids % N_GZ
    offsets = orders // ATOM_DEV
    within = orders % ATOM_DEV
    owner_x = (index_x[:, None] - offsets // 4) % N_GX
    owner_y = (index_y[:, None] - offsets // 2 % 2) % N_GY
    owner_z = (index_z[:, None] - offsets % 2) % N_GZ
    owner = (owner_x * N_GY + owner_y) * N_GZ + owner_z
    atom_ids = owner * ATOM_DEV + within
    positions = jnp.arange(SLOTS)
    return jnp.where(positions[None, :] < live_count[:, None], atom_ids[:, :SLOTS], NATOMS).astype(jnp.int32)


def block_levels(own_key, shape, shards, low, largest):
    def one(axis_at, parts):
        draws = jax.random.uniform(jax.random.fold_in(jax.random.fold_in(own_key, 6), axis_at), (parts,), jnp.float32, low / len(shards), largest / len(shards))
        return jnp.repeat(jnp.exp(draws), shape[axis_at] // parts).reshape((-1,) + (1,) * (len(shape) - axis_at - 1))

    level = one(*shards[0])
    for cut in shards[1:]:
        level = level * one(*cut)
    return level


def noise(rng, shape, deviation, most, cuts=(), held_as=jnp.bfloat16):
    factor_of = block_levels(rng, shape, cuts, -0.22, 0.18) if cuts else 1.0
    values = jax.random.normal(rng, shape, jnp.float32) * deviation * factor_of
    return jnp.minimum(jnp.maximum(values, -most), most).astype(held_as)


def setup_inputs(seed: int = 0) -> dict:
    streams_of = jax.random.split(jax.random.key(seed), 6)
    wavefunctions = noise(streams_of[0], (NNX, NNY, NNZ, WAVES), 1.0, 6.0, ((0, 8), (1, 4), (2, 8)), jnp.float32)
    cell_matrices = noise(streams_of[1], (NCX, NCY, NCZ, CELL_NODES, CELL_NODES), (16 * CELL_NODES) ** -0.5, 0.078125, ((0, 8), (1, 4), (2, 8)))
    projectors = noise(streams_of[2], (DEVICES, SLOTS, NODES_DEV), (1.0 / NODES_DEV ** 0.5), 0.14433756, ((0, 256),), jnp.float32)
    slot_atoms = draw_slot_atoms(jax.random.fold_in(streams_of[5], 71), 0)
    atom_coupling = jnp.clip(jax.random.uniform(streams_of[4], (NATOMS,), jnp.float32, 0.5, 3.0), 0.5, 3.0)
    return dict(wavefunctions=wavefunctions, cell_matrices=cell_matrices, projectors=projectors, slot_atoms=slot_atoms, atom_coupling=atom_coupling)


def extend_global(values, axis_pos):
    first_plane = lax.slice_in_dim(values, 0, 1, axis=axis_pos + 1)
    return jnp.concatenate([values, jnp.roll(first_plane, -1, axis=axis_pos)], axis=axis_pos + 1)


def fold_global(values, axis_pos):
    span_nodes = values.shape[axis_pos + 1]
    inner_part = lax.slice_in_dim(values, 0, span_nodes - 1, axis=axis_pos + 1)
    last_plane = lax.slice_in_dim(values, span_nodes - 1, span_nodes, axis=axis_pos + 1)
    front_plane = lax.slice_in_dim(inner_part, 0, 1, axis=axis_pos + 1) + jnp.roll(last_plane, 1, axis=axis_pos)
    return jnp.concatenate([front_plane, lax.slice_in_dim(inner_part, 1, span_nodes - 1, axis=axis_pos + 1)], axis=axis_pos + 1)


def cell_image(field_now, cell_matrices):
    cells_x, cells_y, cells_z = cell_matrices.shape[0], cell_matrices.shape[1], cell_matrices.shape[2]
    wave_count = field_now.shape[3]
    node_order = field_now.shape[0] // cells_x
    side_nodes = node_order + 1
    rounded = lax.optimization_barrier(field_now.astype(jnp.bfloat16)).astype(jnp.float32)
    values = rounded.reshape(cells_x, node_order, cells_y, node_order, cells_z, node_order, wave_count)
    values = extend_global(values, 0)
    values = extend_global(values, 2)
    values = extend_global(values, 4)
    stacked = values.transpose(0, 2, 4, 1, 3, 5, 6).reshape(cells_x, cells_y, cells_z, side_nodes ** 3, wave_count)
    product = jnp.einsum("xyzmn,xyznw->xyzmw", cell_matrices.astype(jnp.float32), stacked)
    product = product.reshape(cells_x, cells_y, cells_z, side_nodes, side_nodes, side_nodes, wave_count)
    product = product.transpose(0, 3, 1, 4, 2, 5, 6)
    product = fold_global(product, 4)
    product = fold_global(product, 2)
    product = fold_global(product, 0)
    return product.reshape(field_now.shape)


def nonlocal_image(field_now, projectors, slot_atoms, atom_coupling):
    grid_x, grid_y, grid_z, wave_count = field_now.shape
    block_x = grid_x // N_GX
    block_y = grid_y // N_GY
    block_z = grid_z // N_GZ
    blocks = field_now.reshape(N_GX, block_x, N_GY, block_y, N_GZ, block_z, wave_count)
    blocks = blocks.transpose(0, 2, 4, 1, 3, 5, 6).reshape(DEVICES, block_x * block_y * block_z, wave_count)
    coefficients = jnp.einsum("dsn,dnw->dsw", projectors, blocks, precision=lax.Precision.HIGHEST)
    slot_count = projectors.shape[1]
    atom_count = atom_coupling.shape[0]
    flat_coef = coefficients.reshape(DEVICES * slot_count, wave_count)
    columns = jnp.arange(atom_count).astype(jnp.int32)
    selector = (slot_atoms.reshape(-1)[:, None] == columns[None, :]).astype(jnp.float32)
    atom_totals = jnp.dot(selector.T, flat_coef, precision=lax.Precision.HIGHEST)
    weighted = atom_totals * atom_coupling[:, None]
    back = jnp.dot(selector, weighted, precision=lax.Precision.HIGHEST).reshape(DEVICES, slot_count, wave_count)
    image = jnp.einsum("dsn,dsw->dnw", projectors, back, precision=lax.Precision.HIGHEST)
    image = image.reshape(N_GX, N_GY, N_GZ, block_x, block_y, block_z, wave_count).transpose(0, 3, 1, 4, 2, 5, 6)
    return image.reshape(field_now.shape)


def reference(wavefunctions, cell_matrices, projectors, slot_atoms, atom_coupling):
    def apply_operator(field_now):
        return cell_image(field_now, cell_matrices) + nonlocal_image(field_now, projectors, slot_atoms, atom_coupling)

    previous = wavefunctions
    current = apply_operator(wavefunctions)
    for repeat in range(DEGREE - 1):
        following = 2.0 * apply_operator(current) - previous
        previous, current = current, following
    return current
```

```python
import itertools

import jax
import jax.numpy as jnp
from jax import lax
from jax.experimental import pallas as pl
from jax.experimental.pallas import tpu as pltpu
from jax.sharding import PartitionSpec as P

MESH = pl.DeviceIdType.MESH
F32 = jnp.float32
BF16 = jnp.bfloat16

LINES = 169
HALF = LINES * 8
ROWS = 2 * HALF
BLOCK = 104
PAD_NODES = 392

ALL = [d for d in itertools.product((-1, 0, 1), repeat=3) if any(d)]
ALL.sort(key=lambda d: sum(map(abs, d)))
DOWN = [d for d in ALL if max(d) <= 0]
UP = [d for d in ALL if min(d) >= 0]
BITS = [d for d in itertools.product((0, 1), repeat=3) if any(d)]


def kind_of(delta):
    return tuple(int(d != 0) for d in delta)


def message_rows(kind):
    return {
        (1, 0, 0): 208,
        (0, 1, 0): 208,
        (0, 0, 1): 169,
        (1, 1, 0): 16,
        (1, 0, 1): 13,
        (0, 1, 1): 13,
        (1, 1, 1): 1,
    }[kind]


def message_type(kind):
    return F32 if kind == (1, 1, 1) else BF16


def z_row(z):
    return 0 if z == 0 else HALF + 6


def pieces_of(kind, coords):
    x, y, z = coords
    if kind == (1, 0, 0):
        return [(k * HALF + x * BLOCK, BLOCK, 1) for k in (0, 1)]
    if kind == (0, 1, 0):
        return [(k * HALF + (13 * i + y) * 8, 8, 1) for k in (0, 1) for i in range(13)]
    if kind == (0, 0, 1):
        return [(z_row(z), LINES, 8)]
    if kind == (1, 1, 0):
        return [(k * HALF + (13 * x + y) * 8, 8, 1) for k in (0, 1)]
    if kind == (1, 0, 1):
        return [(z_row(z) + x * BLOCK, 13, 8)]
    if kind == (0, 1, 1):
        return [(z_row(z) + y * 8, 13, BLOCK)]
    return [(z_row(z) + (13 * x + y) * 8, 1, 1)]


def rows_at(start, count, stride):
    return pl.ds(start, count) if stride == 1 else pl.ds(start, count, stride)


def packed(field, h, kind, coords):
    parts = [field[h, rows_at(*p), :] for p in pieces_of(kind, coords)]
    return parts[0] if len(parts) == 1 else jnp.concatenate(parts, axis=0)


def merge(field, h, kind, coords, message, adding):
    at = 0
    for start, count, stride in pieces_of(kind, coords):
        part = message[at : at + count]
        rows = rows_at(start, count, stride)
        field[h, rows, :] = field[h, rows, :] + part if adding else part
        at += count


def both_halves(field, rows):
    return jnp.concatenate([field[0, rows, :], field[1, rows, :]], axis=1)


def neighbour(delta):
    out = []
    for name, d in zip(("gx", "gy", "gz"), delta):
        size = lax.axis_size(name)
        out.append((lax.axis_index(name) + d + size) % size)
    return tuple(out)


def start_exchange(field, deltas, send, recv, send_sem, recv_sem):
    copies = []
    for at, delta in enumerate(deltas):
        kind = kind_of(delta)
        coords = tuple(12 if d > 0 else 0 for d in delta)
        for h in (0, 1):
            send[at][h] = packed(field, h, kind, coords).astype(message_type(kind))
        copy = pltpu.make_async_remote_copy(
            src_ref=send[at],
            dst_ref=recv[at],
            send_sem=send_sem.at[at],
            recv_sem=recv_sem.at[at],
            device_id=neighbour(delta),
            device_id_type=MESH,
        )
        copy.start()
        copies.append(copy)
    return copies


def end_exchange(field, deltas, copies, recv, adding):
    for at, delta in enumerate(deltas):
        copies[at].wait_recv()
        coords = tuple(12 if d < 0 else 0 for d in delta)
        for h in (0, 1):
            merge(field, h, kind_of(delta), coords, recv[at][h].astype(F32), adding)


def exact_halves(values):
    high = values.astype(BF16)
    return high, (values - high.astype(F32)).astype(BF16)


def mm(a, b):
    return jnp.dot(a, b, preferred_element_type=F32)


def mm_nt(a, b):
    return lax.dot_general(a, b, (((1,), (1,)), ((), ())), preferred_element_type=F32)


def kernel(w_ref, k_ref, p_ref, slots_ref, coupling_ref, out_ref, *scratch):
    (field, image, pad_k, proj, proj_n, proj_t) = scratch[:6]
    nl_send, nl_recv, nl_own, nl_back, nl_sems = scratch[6:11]
    sems = scratch[11]
    buffers = scratch[12:]
    at = 0
    groups = []
    sem_at = 0
    for deltas in (DOWN, ALL, UP):
        n = len(deltas)
        groups.append(
            (
                buffers[at : at + n],
                buffers[at + n : at + 2 * n],
                sems.at[0, pl.ds(sem_at, n)],
                sems.at[1, pl.ds(sem_at, n)],
            )
        )
        at += 2 * n
        sem_at += n

    barrier = pltpu.get_barrier_semaphore()
    for delta in ALL:
        pl.semaphore_signal(barrier, inc=1, device_id=neighbour(delta), device_id_type=MESH)

    field[...] = jnp.zeros((2, ROWS, 128), F32)

    def spread(x, carry):
        low = w_ref[x, :, 0:8, :]
        high = w_ref[x, :, 8:12, :]
        high = jnp.concatenate([high, high], axis=1)
        row = lax.broadcasted_iota(jnp.int32, (12, 8, 256), 1)
        upper = jnp.where(row < 2, pltpu.roll(low, 2, 1), jnp.where(row < 6, pltpu.roll(high, 2, 1), 0.0))
        base = pl.multiple_of(x * BLOCK, 8)
        for h in (0, 1):
            lanes = slice(128 * h, 128 * h + 128)
            field[h, pl.ds(base, 96), :] = low[:, :, lanes].reshape(96, 128)
            field[h, pl.ds(base + HALF, 96), :] = upper[:, :, lanes].reshape(96, 128)
        return carry

    lax.fori_loop(0, 12, spread, 0)
    pl.semaphore_wait(barrier, len(ALL))
    all_copies = []
    first = start_exchange(field, DOWN, *groups[0])
    all_copies += first

    ids = slots_ref[...]
    owner = ids >> 1
    d_x = (lax.axis_index("gx") - (owner >> 5)) & 7
    d_y = (lax.axis_index("gy") - ((owner >> 3) & 3)) & 3
    d_z = (lax.axis_index("gz") - (owner & 7)) & 7
    place = ((d_x * 2 + d_y) * 2 + d_z) * 2 + (ids & 1)
    place = jnp.where(ids < coupling_ref.shape[0], place, -1)
    order = jnp.broadcast_to(place, (16, 16)) == lax.broadcasted_iota(jnp.int32, (16, 16), 0)
    order = jnp.where(order, 1.0, 0.0).astype(BF16)
    p_high, p_low = exact_halves(p_ref[...])
    proj[...] = jnp.zeros((48, 1920), BF16)
    p_high = mm(order, p_high).astype(BF16)
    p_low = mm(order, p_low).astype(BF16)
    proj[:, pl.ds(0, 1728)] = jnp.concatenate([p_high, p_low, p_high], axis=0)

    def spread_projectors(x, carry):
        begin = pl.multiple_of((x * 144) // 128 * 128, 128)
        window = proj[:, pl.ds(begin, 384)]
        row = lax.broadcasted_iota(jnp.int32, (2 * BLOCK, 1), 0)
        k = jnp.where(row >= BLOCK, 1, 0)
        inner = row - k * BLOCK
        y = inner >> 3
        r = inner & 7
        live = (y < 12) & (r < 7) & ((k == 0) | ((r >= 1) & (r <= 5)))
        target = jnp.where(live, 144 * x - begin + 12 * y + 6 * k + r, -1)
        pick = lax.broadcasted_iota(jnp.int32, (2 * BLOCK, 384), 1) == target
        pick = jnp.where(pick, 1.0, 0.0)
        for half in (0, 1):
            sel = pick[half * BLOCK : (half + 1) * BLOCK].astype(BF16)
            proj_t[half * 12 + x] = mm_nt(sel, window).astype(BF16)
            proj_n[half * 12 + x] = mm_nt(window[0:32], sel).astype(BF16)
        return carry

    lax.fori_loop(0, 12, spread_projectors, 0)

    def block_start(kx):
        return pl.multiple_of((kx // 12) * HALF + (kx % 12) * BLOCK, 8)

    def start_coefficients(values, app):
        def step(kx, total):
            high, low = exact_halves(both_halves(values, pl.ds(block_start(kx), BLOCK)))
            rows = proj_n[kx]
            both = mm(rows, high)
            return total + both[0:16] + both[16:32] + mm(rows[0:16], low)

        total = lax.fori_loop(0, 24, step, jnp.zeros((16, 256), F32))
        for g in range(8):
            nl_send[app, g] = total[2 * g : 2 * g + 2]
        copies = []
        for at, bits in enumerate(BITS):
            copy = pltpu.make_async_remote_copy(
                src_ref=nl_send.at[app, at + 1],
                dst_ref=nl_recv.at[app, at + 1],
                send_sem=nl_sems.at[0, app, at],
                recv_sem=nl_sems.at[1, app, at],
                device_id=neighbour(tuple(-b for b in bits)),
                device_id_type=MESH,
            )
            copy.start()
            copies.append(copy)
        return copies

    def start_totals(app, copies):
        total = nl_send[app, 0]
        for at, copy in enumerate(copies):
            copy.wait_recv()
            total = total + nl_recv[app, at + 1]
        own = ((lax.axis_index("gx") * 4 + lax.axis_index("gy")) * 8 + lax.axis_index("gz")) * 2
        row = lax.broadcasted_iota(jnp.int32, (2, 256), 0)
        weight = jnp.where(row == 0, coupling_ref[own], coupling_ref[own + 1])
        nl_own[app] = total * weight
        out = []
        for at, bits in enumerate(BITS):
            copy = pltpu.make_async_remote_copy(
                src_ref=nl_own.at[app],
                dst_ref=nl_back.at[app, at + 1],
                send_sem=nl_sems.at[0, app, 7 + at],
                recv_sem=nl_sems.at[1, app, 7 + at],
                device_id=neighbour(bits),
                device_id_type=MESH,
            )
            copy.start()
            out.append(copy)
        return out

    def add_nonlocal(total, app, copies):
        parts = [nl_own[app]]
        for at, copy in enumerate(copies):
            copy.wait_recv()
            parts.append(nl_back[app, at + 1])
        high, low = exact_halves(jnp.concatenate(parts, axis=0))
        back = jnp.concatenate([high, high, low], axis=0)

        def step(kx, carry):
            rows = pl.ds(block_start(kx), BLOCK)
            added = mm(proj_t[kx], back)
            for h in (0, 1):
                total[h, rows, :] = total[h, rows, :] + added[:, 128 * h : 128 * h + 128]
            return carry

        lax.fori_loop(0, 24, step, 0)

    def cells(values, total):
        total[...] = jnp.zeros((2, ROWS, 128), F32)

        def step(c, carry):
            base = (c % 2) * HALF + (c // 4) * (6 * BLOCK) + (c // 2 % 2) * 48
            rows = [pl.ds(pl.multiple_of(base + a * BLOCK, 8), 56) for a in range(7)]
            stacked = jnp.concatenate([both_halves(values, r) for r in rows], axis=0).astype(BF16)
            product = mm(pad_k[c], stacked)
            for a in range(7):
                for h in (0, 1):
                    part = product[56 * a : 56 * a + 56, 128 * h : 128 * h + 128]
                    total[h, rows[a], :] = total[h, rows[a], :] + part
            return carry

        lax.fori_loop(0, 8, step, 0)

    def join_middle(total):
        low, high = pl.ds(6, LINES, 8), pl.ds(HALF, LINES, 8)
        for h in (0, 1):
            both = total[h, low, :] + total[h, high, :]
            total[h, low, :] = both
            total[h, high, :] = both

    reduce_1 = start_coefficients(field, 0)
    all_copies += reduce_1

    col = lax.broadcasted_iota(jnp.int32, (343, PAD_NODES), 1)
    node = jnp.where((col & 7) < 7, (col >> 3) * 7 + (col & 7), -1)
    widen = jnp.where(lax.broadcasted_iota(jnp.int32, (343, PAD_NODES), 0) == node, 1.0, 0.0).astype(BF16)
    row = lax.broadcasted_iota(jnp.int32, (PAD_NODES, 343), 0)
    node = jnp.where((row & 7) < 7, (row >> 3) * 7 + (row & 7), -1)
    raise_ = jnp.where(lax.broadcasted_iota(jnp.int32, (PAD_NODES, 343), 1) == node, 1.0, 0.0).astype(BF16)

    def pad_cell(c, carry):
        wide = mm(k_ref[c], widen).astype(BF16)
        pad_k[c] = mm(raise_, wide).astype(BF16)
        return carry

    lax.fori_loop(0, 8, pad_cell, 0)

    totals_1 = start_totals(0, reduce_1)
    all_copies += totals_1
    end_exchange(field, DOWN, first, groups[0][1], False)
    cells(field, image)
    add_nonlocal(image, 0, totals_1)
    join_middle(image)
    middle = start_exchange(image, ALL, *groups[1])
    all_copies += middle
    end_exchange(image, ALL, middle, groups[1][1], True)

    reduce_2 = start_coefficients(image, 1)
    all_copies += reduce_2
    cells(image, field)
    join_middle(field)
    last = start_exchange(field, UP, *groups[2])
    all_copies += last
    totals_2 = start_totals(1, reduce_2)
    all_copies += totals_2
    add_nonlocal(field, 1, totals_2)
    end_exchange(field, UP, last, groups[2][1], True)

    def finish(x, carry):
        base = pl.multiple_of(x * BLOCK, 8)
        low = both_halves(field, pl.ds(base, 96)).reshape(12, 8, 256)
        high = pltpu.roll(both_halves(field, pl.ds(base + HALF, 96)).reshape(12, 8, 256), 6, 1)
        row = lax.broadcasted_iota(jnp.int32, (12, 8, 256), 1)
        out_ref[x, :, 0:8, :] = 2.0 * jnp.where(row < 7, low, high) - w_ref[x, :, 0:8, :]
        out_ref[x, :, 8:12, :] = 2.0 * high[:, 0:4] - w_ref[x, :, 8:12, :]
        return carry

    lax.fori_loop(0, 12, finish, 0)
    for copy in all_copies:
        copy.wait_send()


def local(wavefunctions, cell_matrices, projectors, slot_atoms, atom_coupling):
    buffers = []
    for deltas in (DOWN, ALL, UP):
        one = [
            pltpu.VMEM((2, message_rows(kind_of(d)), 128), message_type(kind_of(d))) for d in deltas
        ]
        buffers += one + one
    count = len(DOWN) + len(ALL) + len(UP)
    vmem = pl.BlockSpec(memory_space=pltpu.VMEM)
    return pl.pallas_call(
        kernel,
        out_shape=jax.ShapeDtypeStruct(wavefunctions.shape, F32),
        in_specs=[vmem, vmem, vmem, vmem, pl.BlockSpec(memory_space=pltpu.SMEM)],
        out_specs=vmem,
        scratch_shapes=[
            pltpu.VMEM((2, ROWS, 128), F32),
            pltpu.VMEM((2, ROWS, 128), F32),
            pltpu.VMEM((8, PAD_NODES, PAD_NODES), BF16),
            pltpu.VMEM((48, 1920), BF16),
            pltpu.VMEM((24, 32, BLOCK), BF16),
            pltpu.VMEM((24, BLOCK, 48), BF16),
            pltpu.VMEM((2, 8, 2, 256), F32),
            pltpu.VMEM((2, 8, 2, 256), F32),
            pltpu.VMEM((2, 2, 256), F32),
            pltpu.VMEM((2, 8, 2, 256), F32),
            pltpu.SemaphoreType.DMA((2, 2, 14)),
            pltpu.SemaphoreType.DMA((2, count)),
            *buffers,
        ],
        compiler_params=pltpu.CompilerParams(collective_id=0, has_side_effects=True, vmem_limit_bytes=60 * 1024 * 1024),
    )(
        wavefunctions,
        cell_matrices.reshape(8, 343, 343),
        projectors[0],
        slot_atoms,
        atom_coupling,
    )


def solution(mesh):
    return jax.shard_map(
        local,
        mesh=mesh,
        in_specs=(
            P("gx", "gy", "gz", None),
            P("gx", "gy", "gz", None, None),
            P(("gx", "gy", "gz"), None, None),
            P(("gx", "gy", "gz"), None),
            P(),
        ),
        out_specs=P("gx", "gy", "gz", None),
        check_vma=False,
    )
```

```python
import itertools

import jax
import jax.numpy as jnp
from jax import lax
from jax.experimental import pallas as pl
from jax.experimental.pallas import tpu as pltpu
from jax.sharding import PartitionSpec as P

MESH = pl.DeviceIdType.MESH
F32 = jnp.float32
BF16 = jnp.bfloat16

LINES = 169
HALF = LINES * 8
ROWS = 2 * HALF
BLOCK = 104
PAIR = 2 * BLOCK
PAD_NODES = 392

ALL = [d for d in itertools.product((-1, 0, 1), repeat=3) if any(d)]
ALL.sort(key=lambda d: sum(map(abs, d)))
DOWN = [d for d in ALL if max(d) <= 0]
UP = [d for d in ALL if min(d) >= 0]
BITS = [d for d in itertools.product((0, 1), repeat=3) if any(d)]


def kind_of(delta):
    return tuple(int(d != 0) for d in delta)


def message_rows(kind):
    return {
        (1, 0, 0): 208,
        (0, 1, 0): 208,
        (0, 0, 1): 169,
        (1, 1, 0): 16,
        (1, 0, 1): 13,
        (0, 1, 1): 13,
        (1, 1, 1): 1,
    }[kind]


def message_type(kind):
    return F32 if kind == (1, 1, 1) else BF16


def z_row(z):
    return 0 if z == 0 else HALF + 6


def pieces_of(kind, coords):
    x, y, z = coords
    if kind == (1, 0, 0):
        return [(k * HALF + x * BLOCK, BLOCK, 1) for k in (0, 1)]
    if kind == (0, 1, 0):
        return [(k * HALF + (13 * i + y) * 8, 8, 1) for k in (0, 1) for i in range(13)]
    if kind == (0, 0, 1):
        return [(z_row(z), LINES, 8)]
    if kind == (1, 1, 0):
        return [(k * HALF + (13 * x + y) * 8, 8, 1) for k in (0, 1)]
    if kind == (1, 0, 1):
        return [(z_row(z) + x * BLOCK, 13, 8)]
    if kind == (0, 1, 1):
        return [(z_row(z) + y * 8, 13, BLOCK)]
    return [(z_row(z) + (13 * x + y) * 8, 1, 1)]


def rows_at(start, count, stride):
    return pl.ds(start, count) if stride == 1 else pl.ds(start, count, stride)


def packed(field, h, kind, coords):
    parts = [field[h, rows_at(*p), :] for p in pieces_of(kind, coords)]
    return parts[0] if len(parts) == 1 else jnp.concatenate(parts, axis=0)


def merge(field, h, kind, coords, message, adding):
    at = 0
    for start, count, stride in pieces_of(kind, coords):
        part = message[at : at + count]
        rows = rows_at(start, count, stride)
        field[h, rows, :] = field[h, rows, :] + part if adding else part
        at += count


def both_halves(field, rows):
    return jnp.concatenate([field[0, rows, :], field[1, rows, :]], axis=1)


def neighbour(delta):
    out = []
    for name, d in zip(("gx", "gy", "gz"), delta):
        size = lax.axis_size(name)
        out.append((lax.axis_index(name) + d + size) % size)
    return tuple(out)


def exchange_copy(at, deltas, send, recv, send_sem, recv_sem):
    return pltpu.make_async_remote_copy(
        src_ref=send[at],
        dst_ref=recv[at],
        send_sem=send_sem.at[at],
        recv_sem=recv_sem.at[at],
        device_id=neighbour(deltas[at]),
        device_id_type=MESH,
    )


def pack_message(field, at, deltas, send):
    kind = kind_of(deltas[at])
    coords = tuple(12 if d > 0 else 0 for d in deltas[at])
    for h in (0, 1):
        send[at][h] = packed(field, h, kind, coords).astype(message_type(kind))


def start_exchange(field, chosen, deltas, group):
    copies = {}
    for at in chosen:
        pack_message(field, at, deltas, group[0])
        copies[at] = exchange_copy(at, deltas, *group)
        copies[at].start()
    return copies


def end_exchange(field, deltas, copies, recv, adding):
    for at, copy in copies.items():
        copy.wait_recv()
        coords = tuple(12 if d < 0 else 0 for d in deltas[at])
        for h in (0, 1):
            merge(field, h, kind_of(deltas[at]), coords, recv[at][h].astype(F32), adding)


def with_z(deltas, z):
    return [at for at, d in enumerate(deltas) if d[2] == z]


def exact_halves(values):
    high = values.astype(BF16)
    return high, (values - high.astype(F32)).astype(BF16)


def mm(a, b):
    return jnp.dot(a, b, preferred_element_type=F32)


def mm_nt(a, b):
    return lax.dot_general(a, b, (((1,), (1,)), ((), ())), preferred_element_type=F32)


def kernel(w_ref, k_ref, p_ref, slots_ref, coupling_ref, out_ref, *scratch):
    (field, image, pad_k, proj, proj_n, proj_t) = scratch[:6]
    nl_send, nl_recv, nl_own, nl_back, nl_sems = scratch[6:11]
    sems = scratch[11]
    buffers = scratch[12:]
    at = 0
    groups = []
    sem_at = 0
    for deltas in (DOWN, ALL, UP):
        n = len(deltas)
        groups.append(
            (
                buffers[at : at + n],
                buffers[at + n : at + 2 * n],
                sems.at[0, pl.ds(sem_at, n)],
                sems.at[1, pl.ds(sem_at, n)],
            )
        )
        at += 2 * n
        sem_at += n

    barrier = pltpu.get_barrier_semaphore()
    for delta in ALL:
        pl.semaphore_signal(barrier, inc=1, device_id=neighbour(delta), device_id_type=MESH)

    field[...] = jnp.zeros((2, ROWS, 128), F32)
    image[...] = jnp.zeros((2, ROWS, 128), F32)

    def spread(x, carry):
        low = w_ref[x, :, 0:8, :]
        high = w_ref[x, :, 8:12, :]
        high = jnp.concatenate([high, high], axis=1)
        row = lax.broadcasted_iota(jnp.int32, (12, 8, 256), 1)
        upper = jnp.where(row < 2, pltpu.roll(low, 2, 1), jnp.where(row < 6, pltpu.roll(high, 2, 1), 0.0))
        base = pl.multiple_of(x * BLOCK, 8)
        for h in (0, 1):
            lanes = slice(128 * h, 128 * h + 128)
            field[h, pl.ds(base, 96), :] = low[:, :, lanes].reshape(96, 128)
            field[h, pl.ds(base + HALF, 96), :] = upper[:, :, lanes].reshape(96, 128)
        return carry

    lax.fori_loop(0, 12, spread, 0)
    for at in range(len(DOWN)):
        pack_message(field, at, DOWN, groups[0][0])

    ids = slots_ref[...]
    owner = ids >> 1
    d_x = (lax.axis_index("gx") - (owner >> 5)) & 7
    d_y = (lax.axis_index("gy") - ((owner >> 3) & 3)) & 3
    d_z = (lax.axis_index("gz") - (owner & 7)) & 7
    place = ((d_x * 2 + d_y) * 2 + d_z) * 2 + (ids & 1)
    place = jnp.where(ids < coupling_ref.shape[0], place, -1)
    order = jnp.broadcast_to(place, (16, 16)) == lax.broadcasted_iota(jnp.int32, (16, 16), 0)
    order = jnp.where(order, 1.0, 0.0).astype(BF16)
    p_high, p_low = exact_halves(p_ref[...])
    p_high = mm(order, p_high)
    p_low = mm(order, p_low)
    proj[:, pl.ds(1664, 256)] = jnp.zeros((48, 256), F32)
    proj[:, pl.ds(0, 1728)] = jnp.concatenate([p_high, p_low, p_high], axis=0)

    def picked(position, k):
        plane = jnp.where(position >= BLOCK, 1, 0)
        inner = position - plane * BLOCK
        y, r = inner >> 3, inner & 7
        live = (y < 12) & ((r < 7) if k == 0 else ((r >= 1) & (r <= 5)))
        return jnp.where(live, 144 * plane + 12 * y + 6 * k + r, -1)

    picks = []
    for k in (0, 1):
        target = picked(lax.broadcasted_iota(jnp.int32, (PAIR, 1), 0), k)
        tall = lax.broadcasted_iota(jnp.int32, (PAIR, 384), 1) == target
        target = picked(lax.broadcasted_iota(jnp.int32, (1, PAIR), 1), k)
        wide = lax.broadcasted_iota(jnp.int32, (384, PAIR), 0) == target
        picks.append([jnp.where(v, 1.0, 0.0).astype(BF16) for v in (tall, wide)])
    for pair in range(6):
        begin = 288 * pair // 128 * 128
        window = proj[:, pl.ds(begin, 384)]
        if begin != 288 * pair:
            window = pltpu.roll(window, 384 - (288 * pair - begin), 1)
        window = window.astype(BF16)
        for k in (0, 1):
            proj_t[6 * k + pair] = mm_nt(picks[k][0], window).astype(BF16)
            proj_n[6 * k + pair] = mm(window[0:32], picks[k][1]).astype(BF16)

    def pair_rows(kp):
        return pl.ds((kp // 6) * HALF + (kp % 6) * PAIR, PAIR)

    def set_coefficients(values, app):
        total = jnp.zeros((16, 256), F32)
        for kp in range(12):
            high, low = exact_halves(both_halves(values, pair_rows(kp)))
            rows = proj_n[kp]
            both = mm(rows, high)
            total = total + (both[0:16] + (both[16:32] + mm(rows[0:16], low)))
        for g in range(8):
            nl_send[app, g] = total[2 * g : 2 * g + 2]

    def start_coefficients(app):
        copies = []
        for at, bits in enumerate(BITS):
            copy = pltpu.make_async_remote_copy(
                src_ref=nl_send.at[app, at + 1],
                dst_ref=nl_recv.at[app, at + 1],
                send_sem=nl_sems.at[0, app, at],
                recv_sem=nl_sems.at[1, app, at],
                device_id=neighbour(tuple(-b for b in bits)),
                device_id_type=MESH,
            )
            copy.start()
            copies.append(copy)
        return copies

    def start_totals(app, copies):
        total = nl_send[app, 0]
        for at, copy in enumerate(copies):
            copy.wait_recv()
            total = total + nl_recv[app, at + 1]
        own = ((lax.axis_index("gx") * 4 + lax.axis_index("gy")) * 8 + lax.axis_index("gz")) * 2
        row = lax.broadcasted_iota(jnp.int32, (2, 256), 0)
        weight = jnp.where(row == 0, coupling_ref[own], coupling_ref[own + 1])
        nl_own[app] = total * weight
        out = []
        for at, bits in enumerate(BITS):
            copy = pltpu.make_async_remote_copy(
                src_ref=nl_own.at[app],
                dst_ref=nl_back.at[app, at + 1],
                send_sem=nl_sems.at[0, app, 7 + at],
                recv_sem=nl_sems.at[1, app, 7 + at],
                device_id=neighbour(bits),
                device_id_type=MESH,
            )
            copy.start()
            out.append(copy)
        return out

    def weighted_totals(app, copies):
        parts = [nl_own[app]]
        for at, copy in enumerate(copies):
            copy.wait_recv()
            parts.append(nl_back[app, at + 1])
        high, low = exact_halves(jnp.concatenate(parts, axis=0))
        return jnp.concatenate([high, high, low], axis=0)

    def add_nonlocal(total, back, k):
        for kp in range(6 * k, 6 * k + 6):
            rows = pair_rows(kp)
            added = mm(proj_t[kp], back)
            for h in (0, 1):
                total[h, rows, :] = total[h, rows, :] + added[:, 128 * h : 128 * h + 128]

    def cells(values, total, k):
        for ij in range(4):
            base = k * HALF + (ij // 2) * (6 * BLOCK) + (ij % 2) * 48
            rows = [pl.ds(base + a * BLOCK, 56) for a in range(7)]
            stacked = jnp.concatenate([both_halves(values, r) for r in rows], axis=0).astype(BF16)
            product = mm(pad_k[2 * ij + k], stacked)
            for a in range(7):
                for h in (0, 1):
                    part = product[56 * a : 56 * a + 56, 128 * h : 128 * h + 128]
                    total[h, rows[a], :] = total[h, rows[a], :] + part

    def join_middle(total):
        low, high = pl.ds(6, LINES, 8), pl.ds(HALF, LINES, 8)
        for h in (0, 1):
            both = total[h, low, :] + total[h, high, :]
            total[h, low, :] = both
            total[h, high, :] = both

    set_coefficients(field, 0)

    pl.semaphore_wait(barrier, len(ALL))
    waits = []
    first = {at: exchange_copy(at, DOWN, *groups[0]) for at in range(len(DOWN))}
    for at in [*with_z(DOWN, -1), *with_z(DOWN, 0)]:
        first[at].start()
    waits += first.values()
    reduce_1 = start_coefficients(0)
    waits += reduce_1

    col = lax.broadcasted_iota(jnp.int32, (343, PAD_NODES), 1)
    node = jnp.where((col & 7) < 7, (col >> 3) * 7 + (col & 7), -1)
    widen = jnp.where(lax.broadcasted_iota(jnp.int32, (343, PAD_NODES), 0) == node, 1.0, 0.0).astype(BF16)
    row = lax.broadcasted_iota(jnp.int32, (PAD_NODES, 686), 0)
    node = jnp.where((row & 7) < 7, 2 * ((row >> 3) * 7 + (row & 7)), -5)
    col = lax.broadcasted_iota(jnp.int32, (PAD_NODES, 686), 1)
    raise_ = [jnp.where(col == node + k, 1.0, 0.0).astype(BF16) for k in (0, 1)]

    def pad_cells(ij, carry):
        pairs = k_ref[ij].reshape(686, 343)
        for k in (0, 1):
            tall = mm(raise_[k], pairs).astype(BF16)
            pad_k[2 * ij + k] = mm(tall, widen).astype(BF16)
        return carry

    lax.fori_loop(0, 4, pad_cells, 0)
    totals_1 = start_totals(0, reduce_1)
    waits += totals_1
    end_exchange(field, DOWN, first, groups[0][1], False)

    cells(field, image, 1)
    middle = start_exchange(image, with_z(ALL, 1), ALL, groups[1])
    cells(field, image, 0)
    back = weighted_totals(0, totals_1)
    add_nonlocal(image, back, 0)
    middle.update(start_exchange(image, with_z(ALL, -1), ALL, groups[1]))
    add_nonlocal(image, back, 1)
    join_middle(image)
    middle.update(start_exchange(image, with_z(ALL, 0), ALL, groups[1]))
    waits += middle.values()
    field[...] = jnp.zeros((2, ROWS, 128), F32)
    end_exchange(image, ALL, middle, groups[1][1], True)

    set_coefficients(image, 1)
    reduce_2 = start_coefficients(1)
    waits += reduce_2
    cells(image, field, 1)
    last = start_exchange(field, with_z(UP, 1), UP, groups[2])
    cells(image, field, 0)
    join_middle(field)
    last.update(start_exchange(field, with_z(UP, 0), UP, groups[2]))
    waits += last.values()
    totals_2 = start_totals(1, reduce_2)
    waits += totals_2
    end_exchange(field, UP, last, groups[2][1], True)
    back = weighted_totals(1, totals_2)

    def finish(pair, carry):
        base = pl.multiple_of(pair * PAIR, 8)
        total = []
        for k in (0, 1):
            total.append(both_halves(field, pl.ds(base + k * HALF, PAIR)) + mm(proj_t[6 * k + pair], back))
        row = lax.broadcasted_iota(jnp.int32, (12, 8, 256), 1)
        for plane in (0, 1):
            x = 2 * pair + plane
            at = plane * BLOCK
            low = total[0][at : at + 96].reshape(12, 8, 256)
            high = pltpu.roll(total[1][at : at + 96].reshape(12, 8, 256), 6, 1)
            out_ref[x, :, 0:8, :] = 2.0 * jnp.where(row < 7, low, high) - w_ref[x, :, 0:8, :]
            out_ref[x, :, 8:12, :] = 2.0 * high[:, 0:4] - w_ref[x, :, 8:12, :]
        return carry

    lax.fori_loop(0, 6, finish, 0)
    for copy in waits:
        copy.wait_send()


def local(wavefunctions, cell_matrices, projectors, slot_atoms, atom_coupling):
    buffers = []
    for deltas in (DOWN, ALL, UP):
        one = [
            pltpu.VMEM((2, message_rows(kind_of(d)), 128), message_type(kind_of(d))) for d in deltas
        ]
        buffers += one + one
    count = len(DOWN) + len(ALL) + len(UP)
    vmem = pl.BlockSpec(memory_space=pltpu.VMEM)
    return pl.pallas_call(
        kernel,
        out_shape=jax.ShapeDtypeStruct(wavefunctions.shape, F32),
        in_specs=[vmem, vmem, vmem, vmem, pl.BlockSpec(memory_space=pltpu.SMEM)],
        out_specs=vmem,
        scratch_shapes=[
            pltpu.VMEM((2, ROWS, 128), F32),
            pltpu.VMEM((2, ROWS, 128), F32),
            pltpu.VMEM((8, PAD_NODES, PAD_NODES), BF16),
            pltpu.VMEM((48, 1920), F32),
            pltpu.VMEM((12, 32, PAIR), BF16),
            pltpu.VMEM((12, PAIR, 48), BF16),
            pltpu.VMEM((2, 8, 2, 256), F32),
            pltpu.VMEM((2, 8, 2, 256), F32),
            pltpu.VMEM((2, 2, 256), F32),
            pltpu.VMEM((2, 8, 2, 256), F32),
            pltpu.SemaphoreType.DMA((2, 2, 14)),
            pltpu.SemaphoreType.DMA((2, count)),
            *buffers,
        ],
        compiler_params=pltpu.CompilerParams(collective_id=0, has_side_effects=True, vmem_limit_bytes=40 * 1024 * 1024),
    )(
        wavefunctions,
        cell_matrices.transpose(0, 1, 3, 2, 4).reshape(4, 343, 2, 343),
        projectors[0],
        slot_atoms,
        atom_coupling,
    )


def solution(mesh):
    return jax.shard_map(
        local,
        mesh=mesh,
        in_specs=(
            P("gx", "gy", "gz", None),
            P("gx", "gy", "gz", None, None),
            P(("gx", "gy", "gz"), None, None),
            P(("gx", "gy", "gz"), None),
            P(),
        ),
        out_specs=P("gx", "gy", "gz", None),
        check_vma=False,
    )
```

```python
import itertools

import jax
import jax.numpy as jnp
from jax import lax
from jax.experimental import pallas as pl
from jax.experimental.pallas import tpu as pltpu
from jax.sharding import PartitionSpec as P

MESH = pl.DeviceIdType.MESH
F32 = jnp.float32
BF16 = jnp.bfloat16

LINES = 169
HALF = LINES * 8
ROWS = 2 * HALF
BLOCK = 104
PAIR = 2 * BLOCK
PAD_NODES = 392

ALL = [d for d in itertools.product((-1, 0, 1), repeat=3) if any(d)]
ALL.sort(key=lambda d: sum(map(abs, d)))
DOWN = [d for d in ALL if max(d) <= 0]
UP = [d for d in ALL if min(d) >= 0]
BITS = [d for d in itertools.product((0, 1), repeat=3) if any(d)]


def kind_of(delta):
    return tuple(int(d != 0) for d in delta)


def message_rows(kind, full):
    return {
        (1, 0, 0): 208,
        (0, 1, 0): 208 if full else 192,
        (0, 0, 1): LINES if full else 156,
        (1, 1, 0): 16,
        (1, 0, 1): 13,
        (0, 1, 1): 13,
        (1, 1, 1): 1,
    }[kind]


def message_type(kind):
    return F32 if kind == (1, 1, 1) else BF16


def z_row(z):
    return 0 if z == 0 else HALF + 6


def pieces_of(kind, coords, full):
    x, y, z = coords
    if kind == (1, 0, 0):
        return [(k * HALF + x * BLOCK, BLOCK, 1) for k in (0, 1)]
    if kind == (0, 1, 0):
        return [(k * HALF + (13 * i + y) * 8, 8, 1) for k in (0, 1) for i in range(13 if full else 12)]
    if kind == (0, 0, 1):
        return [(z_row(z), LINES if full else 156, 8)]
    if kind == (1, 1, 0):
        return [(k * HALF + (13 * x + y) * 8, 8, 1) for k in (0, 1)]
    if kind == (1, 0, 1):
        return [(z_row(z) + x * BLOCK, 13, 8)]
    if kind == (0, 1, 1):
        return [(z_row(z) + y * 8, 13, BLOCK)]
    return [(z_row(z) + (13 * x + y) * 8, 1, 1)]


def rows_at(start, count, stride):
    return pl.ds(start, count) if stride == 1 else pl.ds(start, count, stride)


def packed(field, h, kind, coords, full):
    parts = [field[h, rows_at(*p), :] for p in pieces_of(kind, coords, full)]
    return parts[0] if len(parts) == 1 else jnp.concatenate(parts, axis=0)


def merge(field, h, kind, coords, full, message, adding):
    at = 0
    for start, count, stride in pieces_of(kind, coords, full):
        part = message[at : at + count]
        rows = rows_at(start, count, stride)
        field[h, rows, :] = field[h, rows, :] + part if adding else part
        at += count


def both_halves(field, rows):
    return jnp.concatenate([field[0, rows, :], field[1, rows, :]], axis=1)


def neighbour(delta):
    out = []
    for name, d in zip(("gx", "gy", "gz"), delta):
        size = lax.axis_size(name)
        out.append((lax.axis_index(name) + d + size) % size)
    return tuple(out)


def exchange_copy(at, h, deltas, group):
    send, recv, send_sem, recv_sem = group
    return pltpu.make_async_remote_copy(
        src_ref=send[at].at[h],
        dst_ref=recv[at].at[h],
        send_sem=send_sem.at[at, h],
        recv_sem=recv_sem.at[at, h],
        device_id=neighbour(deltas[at]),
        device_id_type=MESH,
    )


def pack_message(field, at, h, deltas, send):
    kind = kind_of(deltas[at])
    coords = tuple(12 if d > 0 else 0 for d in deltas[at])
    send[at][h] = packed(field, h, kind, coords, deltas is ALL).astype(message_type(kind))


def start_exchange(field, h, chosen, deltas, group):
    copies = {}
    for at in chosen:
        pack_message(field, at, h, deltas, group[0])
        copies[at] = exchange_copy(at, h, deltas, group)
        copies[at].start()
    return copies


def end_exchange(field, h, chosen, deltas, copies, recv, adding):
    for at in chosen:
        copies[at].wait_recv()
        coords = tuple(12 if d < 0 else 0 for d in deltas[at])
        merge(field, h, kind_of(deltas[at]), coords, deltas is ALL, recv[at][h].astype(F32), adding)


def chosen_of(deltas, test):
    return [at for at, d in enumerate(deltas) if test(d)]


def exact_halves(values):
    high = values.astype(BF16)
    return high, (values - high.astype(F32)).astype(BF16)


def mm(a, b):
    return jnp.dot(a, b, preferred_element_type=F32)


def mm_nt(a, b):
    return lax.dot_general(a, b, (((1,), (1,)), ((), ())), preferred_element_type=F32)


def kernel(w_hbm, k_hbm, p_hbm, slots_hbm, coupling_hbm, out_ref, *scratch):
    w_ref, k_ref, p_ref, slots_ref, coupling_ref, in_sems = scratch[:6]
    scratch = scratch[6:]
    (field, image, pad_k, proj, proj_n, proj_t) = scratch[:6]
    nl_send, nl_recv, nl_own, nl_back, nl_sems = scratch[6:11]
    sems = scratch[11]
    buffers = scratch[12:]
    at = 0
    groups = []
    sem_at = 0
    for deltas in (DOWN, ALL, UP):
        n = len(deltas)
        groups.append(
            (
                buffers[at : at + n],
                buffers[at + n : at + 2 * n],
                sems.at[0, pl.ds(sem_at, n)],
                sems.at[1, pl.ds(sem_at, n)],
            )
        )
        at += 2 * n
        sem_at += n

    barrier = pltpu.get_barrier_semaphore()
    for delta in ALL:
        pl.semaphore_signal(barrier, inc=1, device_id=neighbour(delta), device_id_type=MESH)

    inputs = [
        pltpu.make_async_copy(source, target, in_sems.at[at])
        for at, (source, target) in enumerate(
            (
                (w_hbm, w_ref),
                (slots_hbm, slots_ref),
                (p_hbm, p_ref),
                (coupling_hbm, coupling_ref),
                (k_hbm, k_ref),
            )
        )
    ]
    for copy in inputs:
        copy.start()

    for k in (0, 1):
        for x in range(12):
            field[:, pl.ds(k * HALF + (13 * x + 12) * 8, 8), :] = jnp.zeros((2, 8, 128), F32)
    inputs[0].wait()

    def spread(x, carry):
        low = w_ref[x, :, 0:8, :]
        high = w_ref[x, :, 8:12, :]
        high = jnp.concatenate([high, high], axis=1)
        row = lax.broadcasted_iota(jnp.int32, (12, 8, 256), 1)
        upper = jnp.where(row < 2, pltpu.roll(low, 2, 1), jnp.where(row < 6, pltpu.roll(high, 2, 1), 0.0))
        base = pl.multiple_of(x * BLOCK, 8)
        for h in (0, 1):
            lanes = slice(128 * h, 128 * h + 128)
            field[h, pl.ds(base, 96), :] = low[:, :, lanes].reshape(96, 128)
            field[h, pl.ds(base + HALF, 96), :] = upper[:, :, lanes].reshape(96, 128)
        return carry

    lax.fori_loop(0, 12, spread, 0)
    for h in (0, 1):
        for at in range(len(DOWN)):
            pack_message(field, at, h, DOWN, groups[0][0])
    for copy in inputs[1:4]:
        copy.wait()

    ids = slots_ref[...]
    owner = ids >> 1
    d_x = (lax.axis_index("gx") - (owner >> 5)) & 7
    d_y = (lax.axis_index("gy") - ((owner >> 3) & 3)) & 3
    d_z = (lax.axis_index("gz") - (owner & 7)) & 7
    place = ((d_x * 2 + d_y) * 2 + d_z) * 2 + (ids & 1)
    place = jnp.where(ids < coupling_ref.shape[0], place, -1)
    order = jnp.broadcast_to(place, (16, 16)) == lax.broadcasted_iota(jnp.int32, (16, 16), 0)
    order = jnp.where(order, 1.0, 0.0).astype(BF16)
    p_high, p_low = exact_halves(p_ref[...])
    p_high = mm(order, p_high)
    p_low = mm(order, p_low)
    proj[:, pl.ds(1664, 256)] = jnp.zeros((48, 256), F32)
    proj[:, pl.ds(0, 1728)] = jnp.concatenate([p_high, p_low, p_high], axis=0)

    def picked(position, k, twice):
        plane = jnp.where(position >= BLOCK, 1, 0)
        inner = position - plane * BLOCK
        y, r = inner >> 3, inner & 7
        live = (y < 12) & ((r < 7) if k == 0 else ((r >= (0 if twice else 1)) & (r <= 5)))
        return jnp.where(live, 144 * plane + 12 * y + 6 * k + r, -1)

    picks = []
    for k in (0, 1):
        target = picked(lax.broadcasted_iota(jnp.int32, (PAIR, 1), 0), k, True)
        tall = lax.broadcasted_iota(jnp.int32, (PAIR, 384), 1) == target
        target = picked(lax.broadcasted_iota(jnp.int32, (1, PAIR), 1), k, False)
        wide = lax.broadcasted_iota(jnp.int32, (384, PAIR), 0) == target
        picks.append([jnp.where(v, 1.0, 0.0).astype(BF16) for v in (tall, wide)])
    for pair in range(6):
        begin = 288 * pair // 128 * 128
        window = proj[:, pl.ds(begin, 384)]
        if begin != 288 * pair:
            window = pltpu.roll(window, 384 - (288 * pair - begin), 1)
        window = window.astype(BF16)
        for k in (0, 1):
            proj_t[6 * k + pair] = mm_nt(picks[k][0], window).astype(BF16)
            proj_n[6 * k + pair] = mm(window[0:32], picks[k][1]).astype(BF16)

    def pair_rows(kp):
        return pl.ds((kp // 6) * HALF + (kp % 6) * PAIR, PAIR)

    def set_coefficients(values, app, h):
        total = jnp.zeros((16, 128), F32)
        for kp in range(12):
            high, low = exact_halves(values[h, pair_rows(kp), :])
            rows = proj_n[kp]
            both = mm(rows, high)
            total = total + (both[0:16] + (both[16:32] + mm(rows[0:16], low)))
        for g in range(8):
            nl_send[app, g, :, pl.ds(128 * h, 128)] = total[2 * g : 2 * g + 2]

    def start_coefficients(app):
        copies = []
        for at, bits in enumerate(BITS):
            copy = pltpu.make_async_remote_copy(
                src_ref=nl_send.at[app, at + 1],
                dst_ref=nl_recv.at[app, at + 1],
                send_sem=nl_sems.at[0, app, at],
                recv_sem=nl_sems.at[1, app, at],
                device_id=neighbour(tuple(-b for b in bits)),
                device_id_type=MESH,
            )
            copy.start()
            copies.append(copy)
        return copies

    def start_totals(app, copies):
        total = nl_send[app, 0]
        for at, copy in enumerate(copies):
            copy.wait_recv()
            total = total + nl_recv[app, at + 1]
        own = ((lax.axis_index("gx") * 4 + lax.axis_index("gy")) * 8 + lax.axis_index("gz")) * 2
        row = lax.broadcasted_iota(jnp.int32, (2, 256), 0)
        weight = jnp.where(row == 0, coupling_ref[own], coupling_ref[own + 1])
        nl_own[app] = total * weight
        out = []
        for at, bits in enumerate(BITS):
            copy = pltpu.make_async_remote_copy(
                src_ref=nl_own.at[app],
                dst_ref=nl_back.at[app, at + 1],
                send_sem=nl_sems.at[0, app, 7 + at],
                recv_sem=nl_sems.at[1, app, 7 + at],
                device_id=neighbour(bits),
                device_id_type=MESH,
            )
            copy.start()
            out.append(copy)
        return out

    def weighted_totals(app, copies):
        parts = [nl_own[app]]
        for at, copy in enumerate(copies):
            copy.wait_recv()
            parts.append(nl_back[app, at + 1])
        high, low = exact_halves(jnp.concatenate(parts, axis=0))
        return jnp.concatenate([high, high, low], axis=0)

    def add_nonlocal(total, h, back):
        for kp in range(12):
            rows = pair_rows(kp)
            total[h, rows, :] = total[h, rows, :] + mm(proj_t[kp], back[:, 128 * h : 128 * h + 128])

    def cells(values, total, h, k):
        for ij in range(4):
            base = k * HALF + (ij // 2) * (6 * BLOCK) + (ij % 2) * 48
            rows = [pl.ds(base + a * BLOCK, 56) for a in range(7)]
            stacked = jnp.concatenate([values[h, r, :] for r in rows], axis=0).astype(BF16)
            product = mm(pad_k[2 * ij + k], stacked)
            for a in range(7):
                total[h, rows[a], :] = total[h, rows[a], :] + product[56 * a : 56 * a + 56]

    def join_middle(total, h):
        low, high = pl.ds(6, LINES, 8), pl.ds(HALF, LINES, 8)
        both = total[h, low, :] + total[h, high, :]
        total[h, low, :] = both
        total[h, high, :] = both

    for h in (0, 1):
        set_coefficients(field, 0, h)

    pl.semaphore_wait(barrier, len(ALL))
    waits = []
    first = []
    for h in (0, 1):
        first.append({at: exchange_copy(at, h, DOWN, groups[0]) for at in range(len(DOWN))})
        for at in [*chosen_of(DOWN, lambda d: d[2] < 0), *chosen_of(DOWN, lambda d: d[2] == 0)]:
            first[h][at].start()
        waits += first[h].values()
    reduce_1 = start_coefficients(0)
    waits += reduce_1
    image[...] = jnp.zeros((2, ROWS, 128), F32)

    col = lax.broadcasted_iota(jnp.int32, (343, PAD_NODES), 1)
    node = jnp.where((col & 7) < 7, (col >> 3) * 7 + (col & 7), -1)
    widen = jnp.where(lax.broadcasted_iota(jnp.int32, (343, PAD_NODES), 0) == node, 1.0, 0.0).astype(BF16)
    row = lax.broadcasted_iota(jnp.int32, (PAD_NODES, 686), 0)
    node = jnp.where((row & 7) < 7, 2 * ((row >> 3) * 7 + (row & 7)), -5)
    col = lax.broadcasted_iota(jnp.int32, (PAD_NODES, 686), 1)
    raise_ = [jnp.where(col == node + k, 1.0, 0.0).astype(BF16) for k in (0, 1)]

    inputs[4].wait()

    def pad_cells(ij, carry):
        pairs = k_ref[ij].reshape(686, 343)
        for k in (0, 1):
            tall = mm(raise_[k], pairs).astype(BF16)
            pad_k[2 * ij + k] = mm(tall, widen).astype(BF16)
        return carry

    lax.fori_loop(0, 4, pad_cells, 0)
    totals_1 = start_totals(0, reduce_1)
    waits += totals_1

    above = chosen_of(ALL, lambda d: d[2] > 0)
    beside = chosen_of(ALL, lambda d: d[2] == 0 and max(d) > 0)
    below = [at for at in range(len(ALL)) if at not in above and at not in beside]
    owned = chosen_of(ALL, lambda d: min(d) >= 0)
    other = [at for at in range(len(ALL)) if at not in owned]
    everything = range(len(DOWN))
    back = None
    middle = []
    for h in (0, 1):
        end_exchange(field, h, everything, DOWN, first[h], groups[0][1], False)
        cells(field, image, h, 1)
        copies = start_exchange(image, h, above, ALL, groups[1])
        cells(field, image, h, 0)
        join_middle(image, h)
        copies.update(start_exchange(image, h, beside, ALL, groups[1]))
        if back is None:
            back = weighted_totals(0, totals_1)
        add_nonlocal(image, h, back)
        copies.update(start_exchange(image, h, below, ALL, groups[1]))
        middle.append(copies)
        waits += copies.values()
    field[...] = jnp.zeros((2, ROWS, 128), F32)

    last = []
    for h in (0, 1):
        end_exchange(image, h, owned, ALL, middle[h], groups[1][1], True)
        set_coefficients(image, 1, h)
        if h == 1:
            reduce_2 = start_coefficients(1)
            waits += reduce_2
        end_exchange(image, h, other, ALL, middle[h], groups[1][1], True)
        cells(image, field, h, 1)
        copies = start_exchange(field, h, chosen_of(UP, lambda d: d[2] > 0), UP, groups[2])
        cells(image, field, h, 0)
        join_middle(field, h)
        copies.update(start_exchange(field, h, chosen_of(UP, lambda d: d[2] == 0), UP, groups[2]))
        last.append(copies)
        waits += copies.values()
    totals_2 = start_totals(1, reduce_2)
    waits += totals_2
    back = None
    for h in (0, 1):
        end_exchange(field, h, everything, UP, last[h], groups[2][1], True)
        if back is None:
            back = weighted_totals(1, totals_2)
        lanes = slice(128 * h, 128 * h + 128)

        def finish(pair, carry):
            base = pl.multiple_of(pair * PAIR, 8)
            total = []
            for k in (0, 1):
                total.append(field[h, pl.ds(base + k * HALF, PAIR), :] + mm(proj_t[6 * k + pair], back[:, lanes]))
            row = lax.broadcasted_iota(jnp.int32, (12, 8, 128), 1)
            for plane in (0, 1):
                x = 2 * pair + plane
                at = plane * BLOCK
                low = total[0][at : at + 96].reshape(12, 8, 128)
                high = pltpu.roll(total[1][at : at + 96].reshape(12, 8, 128), 6, 1)
                out_ref[x, :, 0:8, lanes] = 2.0 * jnp.where(row < 7, low, high) - w_ref[x, :, 0:8, lanes]
                out_ref[x, :, 8:12, lanes] = 2.0 * high[:, 0:4] - w_ref[x, :, 8:12, lanes]
            return carry

        lax.fori_loop(0, 6, finish, 0)
    for copy in waits:
        copy.wait_send()


def local(wavefunctions, cell_matrices, projectors, slot_atoms, atom_coupling):
    buffers = []
    for deltas in (DOWN, ALL, UP):
        one = [
            pltpu.VMEM((2, message_rows(kind_of(d), deltas is ALL), 128), message_type(kind_of(d)))
            for d in deltas
        ]
        buffers += one + one
    count = len(DOWN) + len(ALL) + len(UP)
    vmem = pl.BlockSpec(memory_space=pltpu.VMEM)
    return pl.pallas_call(
        kernel,
        out_shape=jax.ShapeDtypeStruct(wavefunctions.shape, F32),
        in_specs=[pl.BlockSpec(memory_space=pltpu.HBM)] * 5,
        out_specs=vmem,
        scratch_shapes=[
            pltpu.VMEM((12, 12, 12, 256), F32),
            pltpu.VMEM((4, 343, 2, 343), BF16),
            pltpu.VMEM((16, 1728), F32),
            pltpu.VMEM((1, 16), jnp.int32),
            pltpu.SMEM((512,), F32),
            pltpu.SemaphoreType.DMA((5,)),
            pltpu.VMEM((2, ROWS, 128), F32),
            pltpu.VMEM((2, ROWS, 128), F32),
            pltpu.VMEM((8, PAD_NODES, PAD_NODES), BF16),
            pltpu.VMEM((48, 1920), F32),
            pltpu.VMEM((12, 32, PAIR), BF16),
            pltpu.VMEM((12, PAIR, 48), BF16),
            pltpu.VMEM((2, 8, 2, 256), F32),
            pltpu.VMEM((2, 8, 2, 256), F32),
            pltpu.VMEM((2, 2, 256), F32),
            pltpu.VMEM((2, 8, 2, 256), F32),
            pltpu.SemaphoreType.DMA((2, 2, 14)),
            pltpu.SemaphoreType.DMA((2, count, 2)),
            *buffers,
        ],
        compiler_params=pltpu.CompilerParams(collective_id=0, has_side_effects=True, vmem_limit_bytes=40 * 1024 * 1024),
    )(
        *(
            pltpu.with_memory_space_constraint(array, pltpu.HBM)
            for array in (
                wavefunctions,
                cell_matrices.transpose(0, 1, 3, 2, 4).reshape(4, 343, 2, 343),
                projectors[0],
                slot_atoms,
                atom_coupling,
            )
        )
    )


def solution(mesh):
    return jax.shard_map(
        local,
        mesh=mesh,
        in_specs=(
            P("gx", "gy", "gz", None),
            P("gx", "gy", "gz", None, None),
            P(("gx", "gy", "gz"), None, None),
            P(("gx", "gy", "gz"), None),
            P(),
        ),
        out_specs=P("gx", "gy", "gz", None),
        check_vma=False,
    )
```

```python
import itertools

import jax
import jax.numpy as jnp
from jax import lax
from jax.experimental import pallas as pl
from jax.experimental.pallas import tpu as pltpu
from jax.sharding import PartitionSpec as P

MESH = pl.DeviceIdType.MESH
F32 = jnp.float32
BF16 = jnp.bfloat16

LINES = 169
HALF = LINES * 8
ROWS = 2 * HALF
BLOCK = 104
PAIR = 2 * BLOCK
PAD_NODES = 392

ALL = [d for d in itertools.product((-1, 0, 1), repeat=3) if any(d)]
ALL.sort(key=lambda d: sum(map(abs, d)))
DOWN = [d for d in ALL if max(d) <= 0]
UP = [d for d in ALL if min(d) >= 0]
BITS = [d for d in itertools.product((0, 1), repeat=3) if any(d)]


def kind_of(delta):
    return tuple(int(d != 0) for d in delta)


def message_rows(kind, full):
    return {
        (1, 0, 0): 208,
        (0, 1, 0): 208 if full else 192,
        (0, 0, 1): LINES if full else 156,
        (1, 1, 0): 16,
        (1, 0, 1): 13,
        (0, 1, 1): 13,
        (1, 1, 1): 1,
    }[kind]


def tiled(rows):
    return -(-rows // 16) * 16 if rows > 1 else 1


def message_type(kind):
    return F32 if kind == (1, 1, 1) else BF16


def z_row(z):
    return 0 if z == 0 else HALF + 6


def pieces_of(kind, coords, full):
    x, y, z = coords
    if kind == (1, 0, 0):
        return [(k * HALF + x * BLOCK, BLOCK, 1) for k in (0, 1)]
    if kind == (0, 1, 0):
        return [(k * HALF + (13 * i + y) * 8, 8, 1) for k in (0, 1) for i in range(13 if full else 12)]
    if kind == (0, 0, 1):
        return [(z_row(z), LINES if full else 156, 8)]
    if kind == (1, 1, 0):
        return [(k * HALF + (13 * x + y) * 8, 8, 1) for k in (0, 1)]
    if kind == (1, 0, 1):
        return [(z_row(z) + x * BLOCK, 13, 8)]
    if kind == (0, 1, 1):
        return [(z_row(z) + y * 8, 13, BLOCK)]
    return [(z_row(z) + (13 * x + y) * 8, 1, 1)]


def rows_at(start, count, stride):
    return pl.ds(start, count) if stride == 1 else pl.ds(start, count, stride)


def packed(field, h, kind, coords, full):
    parts = [field[h, rows_at(*p), :] for p in pieces_of(kind, coords, full)]
    return parts[0] if len(parts) == 1 else jnp.concatenate(parts, axis=0)


def merge(field, h, kind, coords, full, message, adding):
    at = 0
    for start, count, stride in pieces_of(kind, coords, full):
        part = message[at : at + count]
        rows = rows_at(start, count, stride)
        field[h, rows, :] = field[h, rows, :] + part if adding else part
        at += count


def both_halves(field, rows):
    return jnp.concatenate([field[0, rows, :], field[1, rows, :]], axis=1)


def neighbour(delta):
    out = []
    for name, d in zip(("gx", "gy", "gz"), delta):
        size = lax.axis_size(name)
        out.append((lax.axis_index(name) + d + size) % size)
    return tuple(out)


def exchange_copy(at, h, deltas, group):
    send, recv, send_sem, recv_sem = group
    return pltpu.make_async_remote_copy(
        src_ref=send[at].at[h],
        dst_ref=recv[at].at[h],
        send_sem=send_sem.at[at, h],
        recv_sem=recv_sem.at[at, h],
        device_id=neighbour(deltas[at]),
        device_id_type=MESH,
    )


def pack_message(field, at, h, deltas, send):
    kind = kind_of(deltas[at])
    coords = tuple(12 if d > 0 else 0 for d in deltas[at])
    value = packed(field, h, kind, coords, deltas is ALL).astype(message_type(kind))
    send[at][h, pl.ds(0, value.shape[0]), :] = value


def start_exchange(field, h, chosen, deltas, group):
    copies = {}
    for at in chosen:
        pack_message(field, at, h, deltas, group[0])
        copies[at] = exchange_copy(at, h, deltas, group)
        copies[at].start()
    return copies


def end_exchange(field, h, chosen, deltas, copies, recv, adding):
    for at in chosen:
        copies[at].wait_recv()
        coords = tuple(12 if d < 0 else 0 for d in deltas[at])
        full = deltas is ALL
        message = recv[at][h, pl.ds(0, message_rows(kind_of(deltas[at]), full)), :].astype(F32)
        merge(field, h, kind_of(deltas[at]), coords, full, message, adding)


def chosen_of(deltas, test):
    return [at for at, d in enumerate(deltas) if test(d)]


def exact_halves(values):
    high = values.astype(BF16)
    return high, (values - high.astype(F32)).astype(BF16)


def mm(a, b):
    return jnp.dot(a, b, preferred_element_type=F32)


def mm_nt(a, b):
    return lax.dot_general(a, b, (((1,), (1,)), ((), ())), preferred_element_type=F32)


def kernel(w_hbm, k_hbm, p_hbm, slots_hbm, coupling_hbm, out_ref, *scratch):
    w_ref, k_ref, p_ref, slots_ref, coupling_ref, in_sems = scratch[:6]
    scratch = scratch[6:]
    (field, image, pad_k, proj, proj_n, proj_t) = scratch[:6]
    loose, scratch = scratch[-1], scratch[:-1]
    nl_send, nl_recv, nl_own, nl_back, nl_sems = scratch[6:11]
    sems = scratch[11]
    buffers = scratch[12:]
    at = 0
    groups = []
    sem_at = 0
    for deltas in (DOWN, ALL, UP):
        n = len(deltas)
        groups.append(
            (
                buffers[at : at + n],
                buffers[at + n : at + 2 * n],
                sems.at[0, pl.ds(sem_at, n)],
                sems.at[1, pl.ds(sem_at, n)],
            )
        )
        at += 2 * n
        sem_at += n

    inputs = [
        pltpu.make_async_copy(source, target, in_sems.at[at])
        for at, (source, target) in enumerate(
            (
                (w_hbm, w_ref),
                (slots_hbm, slots_ref),
                (p_hbm, p_ref),
                (coupling_hbm, coupling_ref),
                (k_hbm, k_ref),
            )
        )
    ]
    for copy in inputs:
        copy.start()

    barrier = pltpu.get_barrier_semaphore()
    for delta in ALL:
        pl.semaphore_signal(barrier, inc=1, device_id=neighbour(delta), device_id_type=MESH)

    for k in (0, 1):
        for x in range(12):
            field[:, pl.ds(k * HALF + (13 * x + 12) * 8, 8), :] = jnp.zeros((2, 8, 128), F32)
    inputs[0].wait()

    def spread(x, carry):
        low = w_ref[x, :, 0:8, :]
        high = w_ref[x, :, 8:12, :]
        high = jnp.concatenate([high, high], axis=1)
        row = lax.broadcasted_iota(jnp.int32, (12, 8, 256), 1)
        upper = jnp.where(row < 2, pltpu.roll(low, 2, 1), jnp.where(row < 6, pltpu.roll(high, 2, 1), 0.0))
        base = pl.multiple_of(x * BLOCK, 8)
        for h in (0, 1):
            lanes = slice(128 * h, 128 * h + 128)
            field[h, pl.ds(base, 96), :] = low[:, :, lanes].reshape(96, 128)
            field[h, pl.ds(base + HALF, 96), :] = upper[:, :, lanes].reshape(96, 128)
        return carry

    lax.fori_loop(0, 12, spread, 0)
    for h in (0, 1):
        for at in range(len(DOWN)):
            pack_message(field, at, h, DOWN, groups[0][0])
    for copy in inputs[1:4]:
        copy.wait()

    ids = slots_ref[...]
    owner = ids >> 1
    d_x = (lax.axis_index("gx") - (owner >> 5)) & 7
    d_y = (lax.axis_index("gy") - ((owner >> 3) & 3)) & 3
    d_z = (lax.axis_index("gz") - (owner & 7)) & 7
    place = ((d_x * 2 + d_y) * 2 + d_z) * 2 + (ids & 1)
    place = jnp.where(ids < coupling_ref.shape[0], place, -1)
    order = jnp.broadcast_to(place, (16, 16)) == lax.broadcasted_iota(jnp.int32, (16, 16), 0)
    order = jnp.where(order, 1.0, 0.0).astype(BF16)
    p_high, p_low = exact_halves(p_ref[...])
    p_high = mm(order, p_high)
    p_low = mm(order, p_low)
    proj[:, pl.ds(1664, 256)] = jnp.zeros((48, 256), F32)
    proj[:, pl.ds(0, 1728)] = jnp.concatenate([p_high, p_low, p_high], axis=0)

    def picked(position, k, twice):
        plane = jnp.where(position >= BLOCK, 1, 0)
        inner = position - plane * BLOCK
        y, r = inner >> 3, inner & 7
        live = (y < 12) & ((r < 7) if k == 0 else ((r >= (0 if twice else 1)) & (r <= 5)))
        return jnp.where(live, 144 * plane + 12 * y + 6 * k + r, -1)

    picks = []
    for k in (0, 1):
        target = picked(lax.broadcasted_iota(jnp.int32, (PAIR, 1), 0), k, True)
        tall = lax.broadcasted_iota(jnp.int32, (PAIR, 384), 1) == target
        target = picked(lax.broadcasted_iota(jnp.int32, (1, PAIR), 1), k, False)
        wide = lax.broadcasted_iota(jnp.int32, (384, PAIR), 0) == target
        picks.append([jnp.where(v, 1.0, 0.0).astype(BF16) for v in (tall, wide)])
    for pair in range(6):
        begin = 288 * pair // 128 * 128
        window = proj[:, pl.ds(begin, 384)]
        if begin != 288 * pair:
            window = pltpu.roll(window, 384 - (288 * pair - begin), 1)
        window = window.astype(BF16)
        for k in (0, 1):
            proj_t[6 * k + pair] = mm_nt(picks[k][0], window).astype(BF16)
            proj_n[6 * k + pair] = mm(window[0:32], picks[k][1]).astype(BF16)

    def pair_rows(kp):
        return pl.ds((kp // 6) * HALF + (kp % 6) * PAIR, PAIR)

    def set_coefficients(values, app, h):
        total = jnp.zeros((16, 128), F32)
        for kp in range(12):
            high, low = exact_halves(values[h, pair_rows(kp), :])
            rows = proj_n[kp]
            both = mm(rows, high)
            total = total + (both[0:16] + (both[16:32] + mm(rows[0:16], low)))
        for g in range(8):
            nl_send[app, g, :, pl.ds(128 * h, 128)] = total[2 * g : 2 * g + 2]

    def start_coefficients(app):
        copies = []
        for at, bits in enumerate(BITS):
            copy = pltpu.make_async_remote_copy(
                src_ref=nl_send.at[app, at + 1],
                dst_ref=nl_recv.at[app, at + 1],
                send_sem=nl_sems.at[0, app, at],
                recv_sem=nl_sems.at[1, app, at],
                device_id=neighbour(tuple(-b for b in bits)),
                device_id_type=MESH,
            )
            copy.start()
            copies.append(copy)
        return copies

    def start_totals(app, copies):
        total = nl_send[app, 0]
        for at, copy in enumerate(copies):
            copy.wait_recv()
            total = total + nl_recv[app, at + 1]
        own = ((lax.axis_index("gx") * 4 + lax.axis_index("gy")) * 8 + lax.axis_index("gz")) * 2
        row = lax.broadcasted_iota(jnp.int32, (2, 256), 0)
        weight = jnp.where(row == 0, coupling_ref[own], coupling_ref[own + 1])
        nl_own[app] = total * weight
        out = []
        for at, bits in enumerate(BITS):
            copy = pltpu.make_async_remote_copy(
                src_ref=nl_own.at[app],
                dst_ref=nl_back.at[app, at + 1],
                send_sem=nl_sems.at[0, app, 7 + at],
                recv_sem=nl_sems.at[1, app, 7 + at],
                device_id=neighbour(bits),
                device_id_type=MESH,
            )
            copy.start()
            out.append(copy)
        return out

    def weighted_totals(app, copies):
        parts = [nl_own[app]]
        for at, copy in enumerate(copies):
            copy.wait_recv()
            parts.append(nl_back[app, at + 1])
        high, low = exact_halves(jnp.concatenate(parts, axis=0))
        return jnp.concatenate([high, high, low], axis=0)

    def add_nonlocal(total, h, back):
        for kp in range(12):
            rows = pair_rows(kp)
            total[h, rows, :] = total[h, rows, :] + mm(proj_t[kp], back[:, 128 * h : 128 * h + 128])

    def cells(values, total, h, k):
        for ij in range(4):
            i, j = ij // 2, ij % 2
            base = k * HALF + i * (6 * BLOCK) + j * 48
            rows = [pl.ds(base + a * BLOCK, 56) for a in range(7)]
            stacked = jnp.concatenate([values[h, r, :] for r in rows], axis=0).astype(BF16)
            product = mm(pad_k[2 * ij + k], stacked)
            for a in range(7):
                shared = 56 if i and a == 0 else 8 if j else 0
                if shared:
                    rows = pl.ds(base + a * BLOCK, shared)
                    total[h, rows, :] = total[h, rows, :] + product[56 * a : 56 * a + shared]
                if shared < 56:
                    rows = pl.ds(base + a * BLOCK + shared, 56 - shared)
                    total[h, rows, :] = product[56 * a + shared : 56 * a + 56]

    def join_middle(total, h):
        low, high = pl.ds(6, LINES, 8), pl.ds(HALF, LINES, 8)
        both = total[h, low, :] + total[h, high, :]
        total[h, low, :] = both
        total[h, high, :] = both

    for h in (0, 1):
        set_coefficients(field, 0, h)

    pl.semaphore_wait(barrier, len(ALL))
    reduce_1 = start_coefficients(0)
    waits = [*reduce_1]
    first = []
    for h in (0, 1):
        first.append({at: exchange_copy(at, h, DOWN, groups[0]) for at in range(len(DOWN))})
        for at in [*chosen_of(DOWN, lambda d: d[2] < 0), *chosen_of(DOWN, lambda d: d[2] == 0)]:
            first[h][at].start()
        waits += first[h].values()

    col = lax.broadcasted_iota(jnp.int32, (343, PAD_NODES), 1)
    node = jnp.where((col & 7) < 7, (col >> 3) * 7 + (col & 7), -1)
    widen = jnp.where(lax.broadcasted_iota(jnp.int32, (343, PAD_NODES), 0) == node, 1.0, 0.0).astype(BF16)
    inputs[4].wait()

    loose[:, pl.ds(680, 24), :] = jnp.zeros((4, 24, 128), F32)

    def pad_cells(ij, carry):
        wide = mm(k_ref[ij].reshape(686, 343), widen)
        for t in range(4):
            width = min(128, PAD_NODES - 128 * t)
            loose[t, pl.ds(0, 686), pl.ds(0, width)] = wide[:, 128 * t : 128 * t + width]
        for t in range(4):
            width = min(128, PAD_NODES - 128 * t)
            for k in (0, 1):
                runs = [loose[t, pl.ds(14 * run + k, 8, 2), :] for run in range(49)]
                tall = jnp.concatenate(runs, axis=0).astype(BF16)
                pad_k[2 * ij + k, :, pl.ds(128 * t, width)] = tall[:, 0:width]
        return carry

    lax.fori_loop(0, 3, pad_cells, 0)
    totals_1 = start_totals(0, reduce_1)
    waits += totals_1
    lax.fori_loop(3, 4, pad_cells, 0)

    above = chosen_of(ALL, lambda d: d[2] > 0)
    beside = chosen_of(ALL, lambda d: d[2] == 0 and max(d) > 0)
    below = [at for at in range(len(ALL)) if at not in above and at not in beside]
    owned = chosen_of(ALL, lambda d: min(d) >= 0)
    other = [at for at in range(len(ALL)) if at not in owned]
    everything = range(len(DOWN))
    middle = []
    for h in (0, 1):
        end_exchange(field, h, everything, DOWN, first[h], groups[0][1], False)
        cells(field, image, h, 1)
        copies = start_exchange(image, h, above, ALL, groups[1])
        cells(field, image, h, 0)
        join_middle(image, h)
        copies.update(start_exchange(image, h, beside, ALL, groups[1]))
        middle.append(copies)
    back = weighted_totals(0, totals_1)
    for h in (0, 1):
        add_nonlocal(image, h, back)
        middle[h].update(start_exchange(image, h, below, ALL, groups[1]))
        waits += middle[h].values()

    last = []
    for h in (0, 1):
        end_exchange(image, h, owned, ALL, middle[h], groups[1][1], True)
        set_coefficients(image, 1, h)
        if h == 1:
            reduce_2 = start_coefficients(1)
            waits += reduce_2
        end_exchange(image, h, other, ALL, middle[h], groups[1][1], True)
        cells(image, field, h, 1)
        copies = start_exchange(field, h, chosen_of(UP, lambda d: d[2] > 0), UP, groups[2])
        if h == 1:
            totals_2 = start_totals(1, reduce_2)
            waits += totals_2
        cells(image, field, h, 0)
        join_middle(field, h)
        copies.update(start_exchange(field, h, chosen_of(UP, lambda d: d[2] == 0), UP, groups[2]))
        last.append(copies)
        waits += copies.values()
    back = None
    for h in (0, 1):
        end_exchange(field, h, everything, UP, last[h], groups[2][1], True)
        if back is None:
            back = weighted_totals(1, totals_2)
        lanes = slice(128 * h, 128 * h + 128)

        def finish(pair, carry):
            base = pl.multiple_of(pair * PAIR, 8)
            total = []
            for k in (0, 1):
                total.append(field[h, pl.ds(base + k * HALF, PAIR), :] + mm(proj_t[6 * k + pair], back[:, lanes]))
            row = lax.broadcasted_iota(jnp.int32, (12, 8, 128), 1)
            for plane in (0, 1):
                x = 2 * pair + plane
                at = plane * BLOCK
                low = total[0][at : at + 96].reshape(12, 8, 128)
                high = pltpu.roll(total[1][at : at + 96].reshape(12, 8, 128), 6, 1)
                out_ref[x, :, 0:8, lanes] = 2.0 * jnp.where(row < 7, low, high) - w_ref[x, :, 0:8, lanes]
                out_ref[x, :, 8:12, lanes] = 2.0 * high[:, 0:4] - w_ref[x, :, 8:12, lanes]
            return carry

        lax.fori_loop(0, 6, finish, 0)
    for copy in waits:
        copy.wait_send()


def local(wavefunctions, cell_matrices, projectors, slot_atoms, atom_coupling):
    buffers = []
    for deltas in (DOWN, ALL, UP):
        one = [
            pltpu.VMEM((2, tiled(message_rows(kind_of(d), deltas is ALL)), 128), message_type(kind_of(d)))
            for d in deltas
        ]
        buffers += one + one
    count = len(DOWN) + len(ALL) + len(UP)
    vmem = pl.BlockSpec(memory_space=pltpu.VMEM)
    return pl.pallas_call(
        kernel,
        out_shape=jax.ShapeDtypeStruct(wavefunctions.shape, F32),
        in_specs=[pl.BlockSpec(memory_space=pltpu.HBM)] * 5,
        out_specs=vmem,
        scratch_shapes=[
            pltpu.VMEM((12, 12, 12, 256), F32),
            pltpu.VMEM((4, 343, 2, 343), BF16),
            pltpu.VMEM((16, 1728), F32),
            pltpu.VMEM((1, 16), jnp.int32),
            pltpu.SMEM((512,), F32),
            pltpu.SemaphoreType.DMA((5,)),
            pltpu.VMEM((2, ROWS, 128), F32),
            pltpu.VMEM((2, ROWS, 128), F32),
            pltpu.VMEM((8, PAD_NODES, PAD_NODES), BF16),
            pltpu.VMEM((48, 1920), F32),
            pltpu.VMEM((12, 32, PAIR), BF16),
            pltpu.VMEM((12, PAIR, 48), BF16),
            pltpu.VMEM((2, 8, 2, 256), F32),
            pltpu.VMEM((2, 8, 2, 256), F32),
            pltpu.VMEM((2, 2, 256), F32),
            pltpu.VMEM((2, 8, 2, 256), F32),
            pltpu.SemaphoreType.DMA((2, 2, 14)),
            pltpu.SemaphoreType.DMA((2, count, 2)),
            *buffers,
            pltpu.VMEM((4, 704, 128), F32),
        ],
        compiler_params=pltpu.CompilerParams(collective_id=0, has_side_effects=True, vmem_limit_bytes=40 * 1024 * 1024),
    )(
        *(
            pltpu.with_memory_space_constraint(array, pltpu.HBM)
            for array in (
                wavefunctions,
                cell_matrices.transpose(0, 1, 3, 2, 4).reshape(4, 343, 2, 343),
                projectors[0],
                slot_atoms,
                atom_coupling,
            )
        )
    )


def solution(mesh):
    return jax.shard_map(
        local,
        mesh=mesh,
        in_specs=(
            P("gx", "gy", "gz", None),
            P("gx", "gy", "gz", None, None),
            P(("gx", "gy", "gz"), None, None),
            P(("gx", "gy", "gz"), None),
            P(),
        ),
        out_specs=P("gx", "gy", "gz", None),
        check_vma=False,
    )
```

```python
import itertools

import jax
import jax.numpy as jnp
from jax import lax
from jax.experimental import pallas as pl
from jax.experimental.pallas import tpu as pltpu
from jax.sharding import PartitionSpec as P

MESH = pl.DeviceIdType.MESH
F32 = jnp.float32
BF16 = jnp.bfloat16

LINES = 169
HALF = LINES * 8
ROWS = 2 * HALF
BLOCK = 104
PAIR = 2 * BLOCK
PAD_NODES = 392

ALL = [d for d in itertools.product((-1, 0, 1), repeat=3) if any(d)]
ALL.sort(key=lambda d: (sum(map(abs, d)), -abs(d[2])))
DOWN = [d for d in ALL if max(d) <= 0]
UP = [d for d in ALL if min(d) >= 0]
BITS = [d for d in itertools.product((0, 1), repeat=3) if any(d)]


def kind_of(delta):
    return tuple(int(d != 0) for d in delta)


def message_rows(kind, full):
    return {
        (1, 0, 0): 208,
        (0, 1, 0): LINES if full else 156,
        (0, 0, 1): LINES if full else 156,
        (1, 1, 0): 16,
        (1, 0, 1): 13,
        (0, 1, 1): 13,
        (1, 1, 1): 1,
    }[kind]


def tiled(rows):
    return -(-rows // 16) * 16 if rows > 1 else 1


def message_type(kind):
    return F32 if kind == (1, 1, 1) else BF16


def z_row(z):
    return 0 if z == 0 else HALF + 6


def pieces_of(kind, coords, full):
    x, y, z = coords
    if kind == (1, 0, 0):
        return [(k * HALF + x * BLOCK, BLOCK, 1) for k in (0, 1)]
    if kind == (0, 1, 0):
        nodes = [*range(7), *range(HALF + 1, HALF + 7)]
        return [(row + y * 8, 13 if full else 12, BLOCK) for row in nodes]
    if kind == (0, 0, 1):
        return [(z_row(z), LINES if full else 156, 8)]
    if kind == (1, 1, 0):
        return [(k * HALF + (13 * x + y) * 8, 8, 1) for k in (0, 1)]
    if kind == (1, 0, 1):
        return [(z_row(z) + x * BLOCK, 13, 8)]
    if kind == (0, 1, 1):
        return [(z_row(z) + y * 8, 13, BLOCK)]
    return [(z_row(z) + (13 * x + y) * 8, 1, 1)]


def rows_at(start, count, stride):
    return pl.ds(start, count) if stride == 1 else pl.ds(start, count, stride)


def packed(field, h, kind, coords, full):
    parts = [field[h, rows_at(*p), :] for p in pieces_of(kind, coords, full)]
    return parts[0] if len(parts) == 1 else jnp.concatenate(parts, axis=0)


def merge(field, h, kind, coords, full, message, adding):
    at = 0
    for start, count, stride in pieces_of(kind, coords, full):
        part = message[at : at + count]
        rows = rows_at(start, count, stride)
        value = field[h, rows, :] + part if adding else part
        field[h, rows, :] = value
        if kind == (0, 1, 0) and start == 6 + 8 * coords[1]:
            field[h, rows_at(start - 6 + HALF, count, stride), :] = value
        at += count


def both_halves(field, rows):
    return jnp.concatenate([field[0, rows, :], field[1, rows, :]], axis=1)


def neighbour(delta):
    out = []
    for name, d in zip(("gx", "gy", "gz"), delta):
        size = lax.axis_size(name)
        out.append((lax.axis_index(name) + d + size) % size)
    return tuple(out)


def exchange_copy(at, h, deltas, group):
    send, recv, send_sem, recv_sem = group
    return pltpu.make_async_remote_copy(
        src_ref=send[at].at[h],
        dst_ref=recv[at].at[h],
        send_sem=send_sem.at[at, h],
        recv_sem=recv_sem.at[at, h],
        device_id=neighbour(deltas[at]),
        device_id_type=MESH,
    )


def pack_message(field, at, h, deltas, send):
    kind = kind_of(deltas[at])
    coords = tuple(12 if d > 0 else 0 for d in deltas[at])
    value = packed(field, h, kind, coords, deltas is ALL).astype(message_type(kind))
    send[at][h, pl.ds(0, value.shape[0]), :] = value


def start_exchange(field, h, chosen, deltas, group):
    copies = {}
    for at in chosen:
        pack_message(field, at, h, deltas, group[0])
        copies[at] = exchange_copy(at, h, deltas, group)
        copies[at].start()
    return copies


def end_exchange(field, h, chosen, deltas, copies, recv, adding):
    for at in sorted(chosen, key=lambda at: abs(deltas[at][2])):
        copies[at].wait_recv()
        coords = tuple(12 if d < 0 else 0 for d in deltas[at])
        full = deltas is ALL
        message = recv[at][h, pl.ds(0, message_rows(kind_of(deltas[at]), full)), :].astype(F32)
        merge(field, h, kind_of(deltas[at]), coords, full, message, adding)


def chosen_of(deltas, test):
    return [at for at, d in enumerate(deltas) if test(d)]


def exact_halves(values):
    high = values.astype(BF16)
    return high, (values - high.astype(F32)).astype(BF16)


def mm(a, b):
    return jnp.dot(a, b, preferred_element_type=F32)


def mm_nt(a, b):
    return lax.dot_general(a, b, (((1,), (1,)), ((), ())), preferred_element_type=F32)


def kernel(w_hbm, k_hbm, p_hbm, slots_hbm, coupling_hbm, out_ref, *scratch):
    w_ref, k_ref, p_ref, slots_ref, coupling_ref, in_sems = scratch[:6]
    scratch = scratch[6:]
    (field, image, pad_k, proj, proj_n, proj_t) = scratch[:6]
    loose, scratch = scratch[-1], scratch[:-1]
    nl_send, nl_recv, nl_own, nl_back, nl_sems = scratch[6:11]
    sems = scratch[11]
    buffers = scratch[12:]
    at = 0
    groups = []
    sem_at = 0
    for deltas in (DOWN, ALL, UP):
        n = len(deltas)
        groups.append(
            (
                buffers[at : at + n],
                buffers[at + n : at + 2 * n],
                sems.at[0, pl.ds(sem_at, n)],
                sems.at[1, pl.ds(sem_at, n)],
            )
        )
        at += 2 * n
        sem_at += n

    inputs = [
        pltpu.make_async_copy(source, target, in_sems.at[at])
        for at, (source, target) in enumerate(
            (
                (w_hbm, w_ref),
                (slots_hbm, slots_ref),
                (p_hbm, p_ref),
                (coupling_hbm, coupling_ref),
                (k_hbm, k_ref),
            )
        )
    ]
    for copy in inputs:
        copy.start()

    barrier = pltpu.get_barrier_semaphore()
    for delta in reversed(ALL):
        pl.semaphore_signal(barrier, inc=1, device_id=neighbour(delta), device_id_type=MESH)

    for k in (0, 1):
        for x in range(12):
            field[:, pl.ds(k * HALF + (13 * x + 12) * 8, 8), :] = jnp.zeros((2, 8, 128), F32)
    inputs[0].wait()

    def spread(x, carry):
        low = w_ref[x, :, 0:8, :]
        high = w_ref[x, :, 8:12, :]
        high = jnp.concatenate([high, high], axis=1)
        row = lax.broadcasted_iota(jnp.int32, (12, 8, 256), 1)
        upper = jnp.where(row < 2, pltpu.roll(low, 2, 1), jnp.where(row < 6, pltpu.roll(high, 2, 1), 0.0))
        base = pl.multiple_of(x * BLOCK, 8)
        for h in (0, 1):
            lanes = slice(128 * h, 128 * h + 128)
            field[h, pl.ds(base, 96), :] = low[:, :, lanes].reshape(96, 128)
            field[h, pl.ds(base + HALF, 96), :] = upper[:, :, lanes].reshape(96, 128)
        return carry

    lax.fori_loop(0, 12, spread, 0)
    for h in (0, 1):
        for at in range(len(DOWN)):
            pack_message(field, at, h, DOWN, groups[0][0])
    for copy in inputs[1:4]:
        copy.wait()

    ids = slots_ref[...]
    owner = ids >> 1
    d_x = (lax.axis_index("gx") - (owner >> 5)) & 7
    d_y = (lax.axis_index("gy") - ((owner >> 3) & 3)) & 3
    d_z = (lax.axis_index("gz") - (owner & 7)) & 7
    place = ((d_x * 2 + d_y) * 2 + d_z) * 2 + (ids & 1)
    place = jnp.where(ids < coupling_ref.shape[0], place, -1)
    order = jnp.broadcast_to(place, (16, 16)) == lax.broadcasted_iota(jnp.int32, (16, 16), 0)
    order = jnp.where(order, 1.0, 0.0).astype(BF16)
    p_high, p_low = exact_halves(p_ref[...])
    p_high = mm(order, p_high)
    p_low = mm(order, p_low)
    proj[:, pl.ds(1664, 256)] = jnp.zeros((48, 256), F32)
    proj[:, pl.ds(0, 1728)] = jnp.concatenate([p_high, p_low, p_high], axis=0)

    def picked(position, k, twice):
        plane = jnp.where(position >= BLOCK, 1, 0)
        inner = position - plane * BLOCK
        y, r = inner >> 3, inner & 7
        live = (y < 12) & ((r < 7) if k == 0 else ((r >= (0 if twice else 1)) & (r <= 5)))
        return jnp.where(live, 144 * plane + 12 * y + 6 * k + r, -1)

    picks = []
    for k in (0, 1):
        target = picked(lax.broadcasted_iota(jnp.int32, (PAIR, 1), 0), k, True)
        tall = lax.broadcasted_iota(jnp.int32, (PAIR, 384), 1) == target
        target = picked(lax.broadcasted_iota(jnp.int32, (1, PAIR), 1), k, False)
        wide = lax.broadcasted_iota(jnp.int32, (384, PAIR), 0) == target
        picks.append([jnp.where(v, 1.0, 0.0).astype(BF16) for v in (tall, wide)])
    for pair in range(6):
        begin = 288 * pair // 128 * 128
        window = proj[:, pl.ds(begin, 384)]
        if begin != 288 * pair:
            window = pltpu.roll(window, 384 - (288 * pair - begin), 1)
        window = window.astype(BF16)
        for k in (0, 1):
            proj_t[6 * k + pair] = mm_nt(picks[k][0], window).astype(BF16)
            proj_n[6 * k + pair] = mm(window[0:32], picks[k][1]).astype(BF16)

    def pair_rows(kp):
        return pl.ds((kp // 6) * HALF + (kp % 6) * PAIR, PAIR)

    def set_coefficients(values, app, h):
        total = jnp.zeros((16, 128), F32)
        for kp in range(12):
            high, low = exact_halves(values[h, pair_rows(kp), :])
            rows = proj_n[kp]
            both = mm(rows, high)
            total = total + (both[0:16] + (both[16:32] + mm(rows[0:16], low)))
        for g in range(8):
            nl_send[app, g, :, pl.ds(128 * h, 128)] = total[2 * g : 2 * g + 2]

    def start_coefficients(app):
        copies = []
        for at, bits in enumerate(BITS):
            copy = pltpu.make_async_remote_copy(
                src_ref=nl_send.at[app, at + 1],
                dst_ref=nl_recv.at[app, at + 1],
                send_sem=nl_sems.at[0, app, at],
                recv_sem=nl_sems.at[1, app, at],
                device_id=neighbour(tuple(-b for b in bits)),
                device_id_type=MESH,
            )
            copy.start()
            copies.append(copy)
        return copies

    def start_totals(app, copies):
        total = nl_send[app, 0]
        for at, copy in enumerate(copies):
            copy.wait_recv()
            total = total + nl_recv[app, at + 1]
        own = ((lax.axis_index("gx") * 4 + lax.axis_index("gy")) * 8 + lax.axis_index("gz")) * 2
        row = lax.broadcasted_iota(jnp.int32, (2, 256), 0)
        weight = jnp.where(row == 0, coupling_ref[own], coupling_ref[own + 1])
        nl_own[app] = total * weight
        out = []
        for at, bits in enumerate(BITS):
            copy = pltpu.make_async_remote_copy(
                src_ref=nl_own.at[app],
                dst_ref=nl_back.at[app, at + 1],
                send_sem=nl_sems.at[0, app, 7 + at],
                recv_sem=nl_sems.at[1, app, 7 + at],
                device_id=neighbour(bits),
                device_id_type=MESH,
            )
            copy.start()
            out.append(copy)
        return out

    def weighted_totals(app, copies):
        parts = [nl_own[app]]
        for at, copy in enumerate(copies):
            copy.wait_recv()
            parts.append(nl_back[app, at + 1])
        high, low = exact_halves(jnp.concatenate(parts, axis=0))
        return jnp.concatenate([high, high, low], axis=0)

    def add_nonlocal(total, h, back):
        for kp in range(12):
            rows = pair_rows(kp)
            total[h, rows, :] = total[h, rows, :] + mm(proj_t[kp], back[:, 128 * h : 128 * h + 128])

    def cells(values, total, h, k):
        for ij in range(4):
            i, j = ij // 2, ij % 2
            base = k * HALF + i * (6 * BLOCK) + j * 48
            rows = [pl.ds(base + a * BLOCK, 56) for a in range(7)]
            stacked = jnp.concatenate([values[h, r, :] for r in rows], axis=0).astype(BF16)
            product = mm(pad_k[2 * ij + k], stacked)
            for a in range(7):
                shared = 56 if i and a == 0 else 8 if j else 0
                if shared:
                    rows = pl.ds(base + a * BLOCK, shared)
                    total[h, rows, :] = total[h, rows, :] + product[56 * a : 56 * a + shared]
                if shared < 56:
                    rows = pl.ds(base + a * BLOCK + shared, 56 - shared)
                    total[h, rows, :] = product[56 * a + shared : 56 * a + 56]

    def join_middle(total, h):
        low, high = pl.ds(6, LINES, 8), pl.ds(HALF, LINES, 8)
        both = total[h, low, :] + total[h, high, :]
        total[h, low, :] = both
        total[h, high, :] = both

    for h in (0, 1):
        set_coefficients(field, 0, h)

    pl.semaphore_wait(barrier, len(ALL))
    reduce_1 = start_coefficients(0)
    waits = [*reduce_1]
    first = []
    for h in (0, 1):
        first.append({at: exchange_copy(at, h, DOWN, groups[0]) for at in range(len(DOWN))})
        for at in [*chosen_of(DOWN, lambda d: d[2] < 0), *chosen_of(DOWN, lambda d: d[2] == 0)]:
            first[h][at].start()
        waits += first[h].values()

    col = lax.broadcasted_iota(jnp.int32, (343, PAD_NODES), 1)
    node = jnp.where((col & 7) < 7, (col >> 3) * 7 + (col & 7), -1)
    widen = jnp.where(lax.broadcasted_iota(jnp.int32, (343, PAD_NODES), 0) == node, 1.0, 0.0).astype(BF16)
    inputs[4].wait()

    loose[:, pl.ds(680, 24), :] = jnp.zeros((4, 24, 128), F32)

    def pad_cells(ij, carry):
        wide = mm(k_ref[ij].reshape(686, 343), widen)
        for t in range(4):
            width = min(128, PAD_NODES - 128 * t)
            loose[t, pl.ds(0, 686), pl.ds(0, width)] = wide[:, 128 * t : 128 * t + width]
        for t in range(4):
            width = min(128, PAD_NODES - 128 * t)
            for k in (0, 1):
                runs = [loose[t, pl.ds(14 * run + k, 8, 2), :] for run in range(49)]
                tall = jnp.concatenate(runs, axis=0).astype(BF16)
                pad_k[2 * ij + k, :, pl.ds(128 * t, width)] = tall[:, 0:width]
        return carry

    lax.fori_loop(0, 3, pad_cells, 0)
    totals_1 = start_totals(0, reduce_1)
    waits += totals_1
    lax.fori_loop(3, 4, pad_cells, 0)

    above = chosen_of(ALL, lambda d: d[2] > 0)
    beside = chosen_of(ALL, lambda d: d[2] == 0 and max(d) > 0)
    below = [at for at in range(len(ALL)) if at not in above and at not in beside]
    owned = chosen_of(ALL, lambda d: min(d) >= 0)
    other = [at for at in range(len(ALL)) if at not in owned]
    everything = range(len(DOWN))
    middle = []
    for h in (0, 1):
        end_exchange(field, h, chosen_of(DOWN, lambda d: d[2] == 0), DOWN, first[h], groups[0][1], False)
        cells(field, image, h, 0)
    for h in (0, 1):
        end_exchange(field, h, chosen_of(DOWN, lambda d: d[2] < 0), DOWN, first[h], groups[0][1], False)
        cells(field, image, h, 1)
        copies = start_exchange(image, h, above, ALL, groups[1])
        join_middle(image, h)
        copies.update(start_exchange(image, h, beside, ALL, groups[1]))
        middle.append(copies)
    back = weighted_totals(0, totals_1)
    for h in (0, 1):
        add_nonlocal(image, h, back)
        middle[h].update(start_exchange(image, h, below, ALL, groups[1]))
        waits += middle[h].values()

    last = []
    for h in (0, 1):
        end_exchange(image, h, owned, ALL, middle[h], groups[1][1], True)
        set_coefficients(image, 1, h)
        if h == 1:
            reduce_2 = start_coefficients(1)
            waits += reduce_2
        end_exchange(image, h, [at for at in other if ALL[at][2] >= 0], ALL, middle[h], groups[1][1], True)
        cells(image, field, h, 0)
        end_exchange(image, h, [at for at in other if ALL[at][2] < 0], ALL, middle[h], groups[1][1], True)
        cells(image, field, h, 1)
        copies = start_exchange(field, h, chosen_of(UP, lambda d: d[2] > 0), UP, groups[2])
        join_middle(field, h)
        copies.update(start_exchange(field, h, chosen_of(UP, lambda d: d[2] == 0), UP, groups[2]))
        if h == 1:
            totals_2 = start_totals(1, reduce_2)
            waits += totals_2
        last.append(copies)
        waits += copies.values()
    back = None
    for h in (0, 1):
        end_exchange(field, h, everything, UP, last[h], groups[2][1], True)
        if back is None:
            back = weighted_totals(1, totals_2)
        lanes = slice(128 * h, 128 * h + 128)

        def finish(pair, carry):
            base = pl.multiple_of(pair * PAIR, 8)
            total = []
            for k in (0, 1):
                total.append(field[h, pl.ds(base + k * HALF, PAIR), :] + mm(proj_t[6 * k + pair], back[:, lanes]))
            row = lax.broadcasted_iota(jnp.int32, (12, 8, 128), 1)
            for plane in (0, 1):
                x = 2 * pair + plane
                at = plane * BLOCK
                low = total[0][at : at + 96].reshape(12, 8, 128)
                high = pltpu.roll(total[1][at : at + 96].reshape(12, 8, 128), 6, 1)
                out_ref[x, :, 0:8, lanes] = 2.0 * jnp.where(row < 7, low, high) - w_ref[x, :, 0:8, lanes]
                out_ref[x, :, 8:12, lanes] = 2.0 * high[:, 0:4] - w_ref[x, :, 8:12, lanes]
            return carry

        lax.fori_loop(0, 6, finish, 0)
    for copy in waits:
        copy.wait_send()


def local(wavefunctions, cell_matrices, projectors, slot_atoms, atom_coupling):
    buffers = []
    for deltas in (DOWN, ALL, UP):
        one = [
            pltpu.VMEM((2, tiled(message_rows(kind_of(d), deltas is ALL)), 128), message_type(kind_of(d)))
            for d in deltas
        ]
        buffers += one + one
    count = len(DOWN) + len(ALL) + len(UP)
    vmem = pl.BlockSpec(memory_space=pltpu.VMEM)
    return pl.pallas_call(
        kernel,
        out_shape=jax.ShapeDtypeStruct(wavefunctions.shape, F32),
        in_specs=[pl.BlockSpec(memory_space=pltpu.HBM)] * 5,
        out_specs=vmem,
        scratch_shapes=[
            pltpu.VMEM((12, 12, 12, 256), F32),
            pltpu.VMEM((4, 343, 2, 343), BF16),
            pltpu.VMEM((16, 1728), F32),
            pltpu.VMEM((1, 16), jnp.int32),
            pltpu.SMEM((512,), F32),
            pltpu.SemaphoreType.DMA((5,)),
            pltpu.VMEM((2, ROWS, 128), F32),
            pltpu.VMEM((2, ROWS, 128), F32),
            pltpu.VMEM((8, PAD_NODES, PAD_NODES), BF16),
            pltpu.VMEM((48, 1920), F32),
            pltpu.VMEM((12, 32, PAIR), BF16),
            pltpu.VMEM((12, PAIR, 48), BF16),
            pltpu.VMEM((2, 8, 2, 256), F32),
            pltpu.VMEM((2, 8, 2, 256), F32),
            pltpu.VMEM((2, 2, 256), F32),
            pltpu.VMEM((2, 8, 2, 256), F32),
            pltpu.SemaphoreType.DMA((2, 2, 14)),
            pltpu.SemaphoreType.DMA((2, count, 2)),
            *buffers,
            pltpu.VMEM((4, 704, 128), F32),
        ],
        compiler_params=pltpu.CompilerParams(collective_id=0, has_side_effects=True, vmem_limit_bytes=40 * 1024 * 1024),
    )(
        *(
            pltpu.with_memory_space_constraint(array, pltpu.HBM)
            for array in (
                wavefunctions,
                cell_matrices.transpose(0, 1, 3, 2, 4).reshape(4, 343, 2, 343),
                projectors[0],
                slot_atoms,
                atom_coupling,
            )
        )
    )


def solution(mesh):
    return jax.shard_map(
        local,
        mesh=mesh,
        in_specs=(
            P("gx", "gy", "gz", None),
            P("gx", "gy", "gz", None, None),
            P(("gx", "gy", "gz"), None, None),
            P(("gx", "gy", "gz"), None),
            P(),
        ),
        out_specs=P("gx", "gy", "gz", None),
        check_vma=False,
    )
```

```python
import itertools

import jax
import jax.numpy as jnp
from jax import lax
from jax.experimental import pallas as pl
from jax.experimental.pallas import tpu as pltpu
from jax.sharding import PartitionSpec as P

MESH = pl.DeviceIdType.MESH
F32 = jnp.float32
BF16 = jnp.bfloat16

LINES = 169
HALF = LINES * 8
ROWS = 2 * HALF
BLOCK = 104
PAIR = 2 * BLOCK
PAD_NODES = 392

ALL = [d for d in itertools.product((-1, 0, 1), repeat=3) if any(d)]
ALL.sort(key=lambda d: (sum(map(abs, d)), -abs(d[2])))
DOWN = [d for d in ALL if max(d) <= 0]
UP = [d for d in ALL if min(d) >= 0]
BITS = [d for d in itertools.product((0, 1), repeat=3) if any(d)]


def kind_of(delta):
    return tuple(int(d != 0) for d in delta)


def message_rows(kind, full):
    return {
        (1, 0, 0): 208,
        (0, 1, 0): LINES if full else 156,
        (0, 0, 1): LINES if full else 156,
        (1, 1, 0): 16,
        (1, 0, 1): 13,
        (0, 1, 1): 13,
        (1, 1, 1): 1,
    }[kind]


def tiled(rows):
    return -(-rows // 16) * 16 if rows > 1 else 1


def message_type(kind):
    return F32 if kind == (1, 1, 1) else BF16


def z_row(z):
    return 0 if z == 0 else HALF + 6


def pieces_of(kind, coords, full):
    x, y, z = coords
    if kind == (1, 0, 0):
        return [(k * HALF + x * BLOCK, BLOCK, 1) for k in (0, 1)]
    if kind == (0, 1, 0):
        nodes = [*range(7), *range(HALF + 1, HALF + 7)]
        return [(row + y * 8, 13 if full else 12, BLOCK) for row in nodes]
    if kind == (0, 0, 1):
        return [(z_row(z), LINES if full else 156, 8)]
    if kind == (1, 1, 0):
        return [(k * HALF + (13 * x + y) * 8, 8, 1) for k in (0, 1)]
    if kind == (1, 0, 1):
        return [(z_row(z) + x * BLOCK, 13, 8)]
    if kind == (0, 1, 1):
        return [(z_row(z) + y * 8, 13, BLOCK)]
    return [(z_row(z) + (13 * x + y) * 8, 1, 1)]


def rows_at(start, count, stride):
    return pl.ds(start, count) if stride == 1 else pl.ds(start, count, stride)


def packed(field, h, kind, coords, full):
    parts = [field[h, rows_at(*p), :] for p in pieces_of(kind, coords, full)]
    return parts[0] if len(parts) == 1 else jnp.concatenate(parts, axis=0)


def merge(field, h, kind, coords, full, message, adding):
    at = 0
    for start, count, stride in pieces_of(kind, coords, full):
        part = message[at : at + count]
        rows = rows_at(start, count, stride)
        value = field[h, rows, :] + part if adding else part
        field[h, rows, :] = value
        if kind == (0, 1, 0) and start == 6 + 8 * coords[1]:
            field[h, rows_at(start - 6 + HALF, count, stride), :] = value
        at += count


def both_halves(field, rows):
    return jnp.concatenate([field[0, rows, :], field[1, rows, :]], axis=1)


def neighbour(delta):
    out = []
    for name, d in zip(("gx", "gy", "gz"), delta):
        size = lax.axis_size(name)
        out.append((lax.axis_index(name) + d + size) % size)
    return tuple(out)


def exchange_copy(at, h, deltas, group):
    send, recv, send_sem, recv_sem = group
    return pltpu.make_async_remote_copy(
        src_ref=send[at].at[h],
        dst_ref=recv[at].at[h],
        send_sem=send_sem.at[at, h],
        recv_sem=recv_sem.at[at, h],
        device_id=neighbour(deltas[at]),
        device_id_type=MESH,
    )


def pack_message(field, at, h, deltas, send):
    kind = kind_of(deltas[at])
    coords = tuple(12 if d > 0 else 0 for d in deltas[at])
    value = packed(field, h, kind, coords, deltas is ALL).astype(message_type(kind))
    send[at][h, pl.ds(0, value.shape[0]), :] = value


def start_exchange(field, h, chosen, deltas, group):
    copies = {}
    for at in chosen:
        pack_message(field, at, h, deltas, group[0])
        copies[at] = exchange_copy(at, h, deltas, group)
        copies[at].start()
    return copies


def end_exchange(field, h, chosen, deltas, copies, recv, adding):
    for at in sorted(chosen, key=lambda at: abs(deltas[at][2])):
        copies[at].wait_recv()
        coords = tuple(12 if d < 0 else 0 for d in deltas[at])
        full = deltas is ALL
        message = recv[at][h, pl.ds(0, message_rows(kind_of(deltas[at]), full)), :].astype(F32)
        merge(field, h, kind_of(deltas[at]), coords, full, message, adding)


def chosen_of(deltas, test):
    return [at for at, d in enumerate(deltas) if test(d)]


def exact_halves(values):
    high = values.astype(BF16)
    return high, (values - high.astype(F32)).astype(BF16)


def mm(a, b):
    return jnp.dot(a, b, preferred_element_type=F32)


def mm_nt(a, b):
    return lax.dot_general(a, b, (((1,), (1,)), ((), ())), preferred_element_type=F32)


def kernel(w_hbm, k_hbm, p_hbm, slots_hbm, coupling_hbm, out_ref, *scratch):
    w_ref, k_ref, p_ref, slots_ref, coupling_ref, in_sems = scratch[:6]
    scratch = scratch[6:]
    (field, image, pad_k, proj, proj_n, proj_t) = scratch[:6]
    loose, scratch = scratch[-1], scratch[:-1]
    nl_send, nl_recv, nl_own, nl_back, nl_sems = scratch[6:11]
    sems = scratch[11]
    buffers = scratch[12:]
    at = 0
    groups = []
    sem_at = 0
    for deltas in (DOWN, ALL, UP):
        n = len(deltas)
        groups.append(
            (
                buffers[at : at + n],
                buffers[at + n : at + 2 * n],
                sems.at[0, pl.ds(sem_at, n)],
                sems.at[1, pl.ds(sem_at, n)],
            )
        )
        at += 2 * n
        sem_at += n

    inputs = [
        pltpu.make_async_copy(source, target, in_sems.at[at])
        for at, (source, target) in enumerate(
            (
                (w_hbm, w_ref),
                (slots_hbm, slots_ref),
                (p_hbm, p_ref),
                (coupling_hbm, coupling_ref),
                (k_hbm, k_ref),
            )
        )
    ]
    for copy in inputs:
        copy.start()

    barrier = pltpu.get_barrier_semaphore()
    for delta in reversed(ALL):
        pl.semaphore_signal(barrier, inc=1, device_id=neighbour(delta), device_id_type=MESH)

    for k in (0, 1):
        for x in range(12):
            field[:, pl.ds(k * HALF + (13 * x + 12) * 8, 8), :] = jnp.zeros((2, 8, 128), F32)
    inputs[0].wait()

    def spread(x, carry):
        low = w_ref[x, :, 0:8, :]
        high = w_ref[x, :, 8:12, :]
        high = jnp.concatenate([high, high], axis=1)
        row = lax.broadcasted_iota(jnp.int32, (12, 8, 256), 1)
        upper = jnp.where(row < 2, pltpu.roll(low, 2, 1), jnp.where(row < 6, pltpu.roll(high, 2, 1), 0.0))
        base = pl.multiple_of(x * BLOCK, 8)
        for h in (0, 1):
            lanes = slice(128 * h, 128 * h + 128)
            field[h, pl.ds(base, 96), :] = low[:, :, lanes].reshape(96, 128)
            field[h, pl.ds(base + HALF, 96), :] = upper[:, :, lanes].reshape(96, 128)
        return carry

    lax.fori_loop(0, 12, spread, 0)
    for h in (0, 1):
        for at in range(len(DOWN)):
            pack_message(field, at, h, DOWN, groups[0][0])
    for copy in inputs[1:4]:
        copy.wait()

    ids = slots_ref[...]
    owner = ids >> 1
    d_x = (lax.axis_index("gx") - (owner >> 5)) & 7
    d_y = (lax.axis_index("gy") - ((owner >> 3) & 3)) & 3
    d_z = (lax.axis_index("gz") - (owner & 7)) & 7
    place = ((d_x * 2 + d_y) * 2 + d_z) * 2 + (ids & 1)
    place = jnp.where(ids < coupling_ref.shape[0], place, -1)
    order = jnp.broadcast_to(place, (16, 16)) == lax.broadcasted_iota(jnp.int32, (16, 16), 0)
    order = jnp.where(order, 1.0, 0.0).astype(BF16)
    p_high, p_low = exact_halves(p_ref[...])
    p_high = mm(order, p_high)
    p_low = mm(order, p_low)
    proj[:, pl.ds(1664, 256)] = jnp.zeros((48, 256), F32)
    proj[:, pl.ds(0, 1728)] = jnp.concatenate([p_high, p_low, p_high], axis=0)

    def picked(position, k, twice):
        plane = jnp.where(position >= BLOCK, 1, 0)
        inner = position - plane * BLOCK
        y, r = inner >> 3, inner & 7
        live = (y < 12) & ((r < 7) if k == 0 else ((r >= (0 if twice else 1)) & (r <= 5)))
        return jnp.where(live, 144 * plane + 12 * y + 6 * k + r, -1)

    picks = []
    for k in (0, 1):
        target = picked(lax.broadcasted_iota(jnp.int32, (PAIR, 1), 0), k, True)
        tall = lax.broadcasted_iota(jnp.int32, (PAIR, 384), 1) == target
        target = picked(lax.broadcasted_iota(jnp.int32, (1, PAIR), 1), k, False)
        wide = lax.broadcasted_iota(jnp.int32, (384, PAIR), 0) == target
        picks.append([jnp.where(v, 1.0, 0.0).astype(BF16) for v in (tall, wide)])
    for pair in range(6):
        begin = 288 * pair // 128 * 128
        window = proj[:, pl.ds(begin, 384)]
        if begin != 288 * pair:
            window = pltpu.roll(window, 384 - (288 * pair - begin), 1)
        window = window.astype(BF16)
        for k in (0, 1):
            proj_t[6 * k + pair] = mm_nt(picks[k][0], window).astype(BF16)
            proj_n[6 * k + pair] = mm(window[0:32], picks[k][1]).astype(BF16)

    def pair_rows(kp):
        return pl.ds((kp // 6) * HALF + (kp % 6) * PAIR, PAIR)

    def set_coefficients(values, app, h):
        total = jnp.zeros((16, 128), F32)
        for kp in range(12):
            high, low = exact_halves(values[h, pair_rows(kp), :])
            rows = proj_n[kp]
            both = mm(rows, high)
            total = total + (both[0:16] + (both[16:32] + mm(rows[0:16], low)))
        for g in range(8):
            nl_send[app, g, :, pl.ds(128 * h, 128)] = total[2 * g : 2 * g + 2]

    def start_coefficients(app):
        copies = []
        for at, bits in enumerate(BITS):
            copy = pltpu.make_async_remote_copy(
                src_ref=nl_send.at[app, at + 1],
                dst_ref=nl_recv.at[app, at + 1],
                send_sem=nl_sems.at[0, app, at],
                recv_sem=nl_sems.at[1, app, at],
                device_id=neighbour(tuple(-b for b in bits)),
                device_id_type=MESH,
            )
            copy.start()
            copies.append(copy)
        return copies

    def start_totals(app, copies):
        total = nl_send[app, 0]
        for at, copy in enumerate(copies):
            copy.wait_recv()
            total = total + nl_recv[app, at + 1]
        own = ((lax.axis_index("gx") * 4 + lax.axis_index("gy")) * 8 + lax.axis_index("gz")) * 2
        row = lax.broadcasted_iota(jnp.int32, (2, 256), 0)
        weight = jnp.where(row == 0, coupling_ref[own], coupling_ref[own + 1])
        nl_own[app] = total * weight
        out = []
        for at, bits in enumerate(BITS):
            copy = pltpu.make_async_remote_copy(
                src_ref=nl_own.at[app],
                dst_ref=nl_back.at[app, at + 1],
                send_sem=nl_sems.at[0, app, 7 + at],
                recv_sem=nl_sems.at[1, app, 7 + at],
                device_id=neighbour(bits),
                device_id_type=MESH,
            )
            copy.start()
            out.append(copy)
        return out

    def weighted_totals(app, copies):
        parts = [nl_own[app]]
        for at, copy in enumerate(copies):
            copy.wait_recv()
            parts.append(nl_back[app, at + 1])
        high, low = exact_halves(jnp.concatenate(parts, axis=0))
        return jnp.concatenate([high, high, low], axis=0)

    def add_nonlocal(total, h, back):
        for kp in range(12):
            rows = pair_rows(kp)
            total[h, rows, :] = total[h, rows, :] + mm(proj_t[kp], back[:, 128 * h : 128 * h + 128])

    def cells(values, total, h, k):
        for ij in range(4):
            i, j = ij // 2, ij % 2
            base = k * HALF + i * (6 * BLOCK) + j * 48
            rows = [pl.ds(base + a * BLOCK, 56) for a in range(7)]
            stacked = jnp.concatenate([values[h, r, :] for r in rows], axis=0).astype(BF16)
            product = mm(pad_k[2 * ij + k], stacked)
            for a in range(7):
                shared = 56 if i and a == 0 else 8 if j else 0
                if shared:
                    rows = pl.ds(base + a * BLOCK, shared)
                    total[h, rows, :] = total[h, rows, :] + product[56 * a : 56 * a + shared]
                if shared < 56:
                    rows = pl.ds(base + a * BLOCK + shared, 56 - shared)
                    total[h, rows, :] = product[56 * a + shared : 56 * a + 56]

    def join_middle(total, h):
        low, high = pl.ds(6, LINES, 8), pl.ds(HALF, LINES, 8)
        both = total[h, low, :] + total[h, high, :]
        total[h, low, :] = both
        total[h, high, :] = both

    for h in (0, 1):
        set_coefficients(field, 0, h)

    pl.semaphore_wait(barrier, len(ALL))
    reduce_1 = start_coefficients(0)
    waits = [*reduce_1]
    first = []
    for h in (0, 1):
        first.append({at: exchange_copy(at, h, DOWN, groups[0]) for at in range(len(DOWN))})
        for at in [*chosen_of(DOWN, lambda d: d[2] < 0), *chosen_of(DOWN, lambda d: d[2] == 0)]:
            first[h][at].start()
        waits += first[h].values()

    col = lax.broadcasted_iota(jnp.int32, (343, PAD_NODES), 1)
    node = jnp.where((col & 7) < 7, (col >> 3) * 7 + (col & 7), -1)
    widen = jnp.where(lax.broadcasted_iota(jnp.int32, (343, PAD_NODES), 0) == node, 1.0, 0.0).astype(BF16)
    inputs[4].wait()

    loose[:, pl.ds(680, 24), :] = jnp.zeros((4, 24, 128), F32)

    def pad_cells(ij, carry):
        wide = mm(k_ref[ij].reshape(686, 343), widen)
        for t in range(4):
            width = min(128, PAD_NODES - 128 * t)
            loose[t, pl.ds(0, 686), pl.ds(0, width)] = wide[:, 128 * t : 128 * t + width]
        for t in range(4):
            width = min(128, PAD_NODES - 128 * t)
            for k in (0, 1):
                runs = [loose[t, pl.ds(14 * run + k, 8, 2), :] for run in range(49)]
                tall = jnp.concatenate(runs, axis=0).astype(BF16)
                pad_k[2 * ij + k, :, pl.ds(128 * t, width)] = tall[:, 0:width]
        return carry

    lax.fori_loop(0, 3, pad_cells, 0)
    totals_1 = start_totals(0, reduce_1)
    waits += totals_1
    lax.fori_loop(3, 4, pad_cells, 0)

    above = chosen_of(ALL, lambda d: d[2] > 0)
    beside = chosen_of(ALL, lambda d: d[2] == 0 and max(d) > 0)
    below = [at for at in range(len(ALL)) if at not in above and at not in beside]
    owned = chosen_of(ALL, lambda d: min(d) >= 0)
    other = [at for at in range(len(ALL)) if at not in owned]
    everything = range(len(DOWN))
    middle = []
    for h in (0, 1):
        end_exchange(field, h, chosen_of(DOWN, lambda d: d[2] == 0), DOWN, first[h], groups[0][1], False)
        cells(field, image, h, 0)
    for h in (0, 1):
        end_exchange(field, h, chosen_of(DOWN, lambda d: d[2] < 0), DOWN, first[h], groups[0][1], False)
        cells(field, image, h, 1)
        copies = start_exchange(image, h, above, ALL, groups[1])
        join_middle(image, h)
        copies.update(start_exchange(image, h, beside, ALL, groups[1]))
        middle.append(copies)
    back = weighted_totals(0, totals_1)
    for h in (0, 1):
        add_nonlocal(image, h, back)
        middle[h].update(start_exchange(image, h, below, ALL, groups[1]))
        waits += middle[h].values()

    last = []
    for h in (0, 1):
        end_exchange(image, h, owned, ALL, middle[h], groups[1][1], True)
        set_coefficients(image, 1, h)
    reduce_2 = start_coefficients(1)
    waits += reduce_2
    for h in (0, 1):
        end_exchange(image, h, [at for at in other if ALL[at][2] >= 0], ALL, middle[h], groups[1][1], True)
        cells(image, field, h, 0)
        end_exchange(image, h, [at for at in other if ALL[at][2] < 0], ALL, middle[h], groups[1][1], True)
        cells(image, field, h, 1)
        copies = start_exchange(field, h, chosen_of(UP, lambda d: d[2] > 0), UP, groups[2])
        join_middle(field, h)
        copies.update(start_exchange(field, h, chosen_of(UP, lambda d: d[2] == 0), UP, groups[2]))
        if h == 0:
            totals_2 = start_totals(1, reduce_2)
            waits += totals_2
        last.append(copies)
        waits += copies.values()
    back = None
    for h in (0, 1):
        end_exchange(field, h, everything, UP, last[h], groups[2][1], True)
        if back is None:
            back = weighted_totals(1, totals_2)
        lanes = slice(128 * h, 128 * h + 128)

        def finish(pair, carry):
            base = pl.multiple_of(pair * PAIR, 8)
            total = []
            for k in (0, 1):
                total.append(field[h, pl.ds(base + k * HALF, PAIR), :] + mm(proj_t[6 * k + pair], back[:, lanes]))
            row = lax.broadcasted_iota(jnp.int32, (12, 8, 128), 1)
            for plane in (0, 1):
                x = 2 * pair + plane
                at = plane * BLOCK
                low = total[0][at : at + 96].reshape(12, 8, 128)
                high = pltpu.roll(total[1][at : at + 96].reshape(12, 8, 128), 6, 1)
                out_ref[x, :, 0:8, lanes] = 2.0 * jnp.where(row < 7, low, high) - w_ref[x, :, 0:8, lanes]
                out_ref[x, :, 8:12, lanes] = 2.0 * high[:, 0:4] - w_ref[x, :, 8:12, lanes]
            return carry

        lax.fori_loop(0, 6, finish, 0)
    for copy in waits:
        copy.wait_send()


def local(wavefunctions, cell_matrices, projectors, slot_atoms, atom_coupling):
    buffers = []
    for deltas in (DOWN, ALL, UP):
        one = [
            pltpu.VMEM((2, tiled(message_rows(kind_of(d), deltas is ALL)), 128), message_type(kind_of(d)))
            for d in deltas
        ]
        buffers += one + one
    count = len(DOWN) + len(ALL) + len(UP)
    vmem = pl.BlockSpec(memory_space=pltpu.VMEM)
    return pl.pallas_call(
        kernel,
        out_shape=jax.ShapeDtypeStruct(wavefunctions.shape, F32),
        in_specs=[pl.BlockSpec(memory_space=pltpu.HBM)] * 5,
        out_specs=vmem,
        scratch_shapes=[
            pltpu.VMEM((12, 12, 12, 256), F32),
            pltpu.VMEM((4, 343, 2, 343), BF16),
            pltpu.VMEM((16, 1728), F32),
            pltpu.VMEM((1, 16), jnp.int32),
            pltpu.SMEM((512,), F32),
            pltpu.SemaphoreType.DMA((5,)),
            pltpu.VMEM((2, ROWS, 128), F32),
            pltpu.VMEM((2, ROWS, 128), F32),
            pltpu.VMEM((8, PAD_NODES, PAD_NODES), BF16),
            pltpu.VMEM((48, 1920), F32),
            pltpu.VMEM((12, 32, PAIR), BF16),
            pltpu.VMEM((12, PAIR, 48), BF16),
            pltpu.VMEM((2, 8, 2, 256), F32),
            pltpu.VMEM((2, 8, 2, 256), F32),
            pltpu.VMEM((2, 2, 256), F32),
            pltpu.VMEM((2, 8, 2, 256), F32),
            pltpu.SemaphoreType.DMA((2, 2, 14)),
            pltpu.SemaphoreType.DMA((2, count, 2)),
            *buffers,
            pltpu.VMEM((4, 704, 128), F32),
        ],
        compiler_params=pltpu.CompilerParams(collective_id=0, has_side_effects=True, vmem_limit_bytes=40 * 1024 * 1024),
    )(
        *(
            pltpu.with_memory_space_constraint(array, pltpu.HBM)
            for array in (
                wavefunctions,
                cell_matrices.transpose(0, 1, 3, 2, 4).reshape(4, 343, 2, 343),
                projectors[0],
                slot_atoms,
                atom_coupling,
            )
        )
    )


def solution(mesh):
    return jax.shard_map(
        local,
        mesh=mesh,
        in_specs=(
            P("gx", "gy", "gz", None),
            P("gx", "gy", "gz", None, None),
            P(("gx", "gy", "gz"), None, None),
            P(("gx", "gy", "gz"), None),
            P(),
        ),
        out_specs=P("gx", "gy", "gz", None),
        check_vma=False,
    )
```

```python
import itertools

import jax
import jax.numpy as jnp
from jax import lax
from jax.experimental import pallas as pl
from jax.experimental.pallas import tpu as pltpu
from jax.sharding import PartitionSpec as P

MESH = pl.DeviceIdType.MESH
F32 = jnp.float32
BF16 = jnp.bfloat16

LINES = 169
HALF = LINES * 8
ROWS = 2 * HALF
BLOCK = 104
PAIR = 2 * BLOCK
PAD_NODES = 392

ALL = [d for d in itertools.product((-1, 0, 1), repeat=3) if any(d)]
ALL.sort(key=lambda d: (sum(map(abs, d)), -abs(d[2])))
DOWN = [d for d in ALL if max(d) <= 0]
UP = [d for d in ALL if min(d) >= 0]
BITS = [d for d in itertools.product((0, 1), repeat=3) if any(d)]


def kind_of(delta):
    return tuple(int(d != 0) for d in delta)


def message_rows(kind, full):
    return {
        (1, 0, 0): 208,
        (0, 1, 0): LINES if full else 156,
        (0, 0, 1): LINES if full else 156,
        (1, 1, 0): 16,
        (1, 0, 1): 13,
        (0, 1, 1): 13,
        (1, 1, 1): 1,
    }[kind]


def tiled(rows):
    return -(-rows // 16) * 16 if rows > 1 else 1


def message_type(kind):
    return F32 if kind == (1, 1, 1) else BF16


def z_row(z):
    return 0 if z == 0 else HALF + 6


def pieces_of(kind, coords, full):
    x, y, z = coords
    if kind == (1, 0, 0):
        return [(k * HALF + x * BLOCK, BLOCK, 1) for k in (0, 1)]
    if kind == (0, 1, 0):
        nodes = [*range(7), *range(HALF + 1, HALF + 7)]
        return [(row + y * 8, 13 if full else 12, BLOCK) for row in nodes]
    if kind == (0, 0, 1):
        return [(z_row(z), LINES if full else 156, 8)]
    if kind == (1, 1, 0):
        return [(k * HALF + (13 * x + y) * 8, 8, 1) for k in (0, 1)]
    if kind == (1, 0, 1):
        return [(z_row(z) + x * BLOCK, 13, 8)]
    if kind == (0, 1, 1):
        return [(z_row(z) + y * 8, 13, BLOCK)]
    return [(z_row(z) + (13 * x + y) * 8, 1, 1)]


def rows_at(start, count, stride):
    return pl.ds(start, count) if stride == 1 else pl.ds(start, count, stride)


def packed(field, h, kind, coords, full):
    parts = [field[h, rows_at(*p), :] for p in pieces_of(kind, coords, full)]
    return parts[0] if len(parts) == 1 else jnp.concatenate(parts, axis=0)


def merge(field, h, kind, coords, full, message, adding):
    at = 0
    for start, count, stride in pieces_of(kind, coords, full):
        part = message[at : at + count]
        rows = rows_at(start, count, stride)
        value = field[h, rows, :] + part if adding else part
        field[h, rows, :] = value
        if kind == (0, 1, 0) and start == 6 + 8 * coords[1]:
            field[h, rows_at(start - 6 + HALF, count, stride), :] = value
        at += count


def both_halves(field, rows):
    return jnp.concatenate([field[0, rows, :], field[1, rows, :]], axis=1)


def neighbour(delta):
    out = []
    for name, d in zip(("gx", "gy", "gz"), delta):
        size = lax.axis_size(name)
        out.append((lax.axis_index(name) + d + size) % size)
    return tuple(out)


def exchange_copy(at, h, deltas, group):
    send, recv, send_sem, recv_sem = group
    return pltpu.make_async_remote_copy(
        src_ref=send[at].at[h],
        dst_ref=recv[at].at[h],
        send_sem=send_sem.at[at, h],
        recv_sem=recv_sem.at[at, h],
        device_id=neighbour(deltas[at]),
        device_id_type=MESH,
    )


def pack_message(field, at, h, deltas, send):
    kind = kind_of(deltas[at])
    coords = tuple(12 if d > 0 else 0 for d in deltas[at])
    value = packed(field, h, kind, coords, deltas is ALL).astype(message_type(kind))
    send[at][h, pl.ds(0, value.shape[0]), :] = value


def start_exchange(field, h, chosen, deltas, group):
    copies = {}
    for at in chosen:
        pack_message(field, at, h, deltas, group[0])
        copies[at] = exchange_copy(at, h, deltas, group)
        copies[at].start()
    return copies


def end_exchange(field, h, chosen, deltas, copies, recv, adding):
    for at in sorted(chosen, key=lambda at: abs(deltas[at][2])):
        copies[at].wait_recv()
        coords = tuple(12 if d < 0 else 0 for d in deltas[at])
        full = deltas is ALL
        message = recv[at][h, pl.ds(0, message_rows(kind_of(deltas[at]), full)), :].astype(F32)
        merge(field, h, kind_of(deltas[at]), coords, full, message, adding)


def chosen_of(deltas, test):
    return [at for at, d in enumerate(deltas) if test(d)]


def exact_halves(values):
    high = values.astype(BF16)
    return high, (values - high.astype(F32)).astype(BF16)


def mm(a, b):
    return jnp.dot(a, b, preferred_element_type=F32)


def mm_nt(a, b):
    return lax.dot_general(a, b, (((1,), (1,)), ((), ())), preferred_element_type=F32)


def kernel(w_hbm, k_hbm, p_hbm, slots_hbm, coupling_hbm, out_ref, *scratch):
    w_ref, k_ref, p_ref, slots_ref, coupling_ref, in_sems = scratch[:6]
    scratch = scratch[6:]
    (field, image, pad_k, proj, proj_n, proj_t) = scratch[:6]
    loose, scratch = scratch[-1], scratch[:-1]
    nl_send, nl_recv, nl_own, nl_back, nl_sems = scratch[6:11]
    sems = scratch[11]
    buffers = scratch[12:]
    at = 0
    groups = []
    sem_at = 0
    for deltas in (DOWN, ALL, UP):
        n = len(deltas)
        groups.append(
            (
                buffers[at : at + n],
                buffers[at + n : at + 2 * n],
                sems.at[0, pl.ds(sem_at, n)],
                sems.at[1, pl.ds(sem_at, n)],
            )
        )
        at += 2 * n
        sem_at += n

    inputs = [
        pltpu.make_async_copy(source, target, in_sems.at[at])
        for at, (source, target) in enumerate(
            (
                (w_hbm, w_ref),
                (slots_hbm, slots_ref),
                (p_hbm, p_ref),
                (coupling_hbm, coupling_ref),
                (k_hbm, k_ref),
            )
        )
    ]
    for copy in inputs:
        copy.start()

    barrier = pltpu.get_barrier_semaphore()
    for delta in reversed(ALL):
        pl.semaphore_signal(barrier, inc=1, device_id=neighbour(delta), device_id_type=MESH)

    for k in (0, 1):
        for x in range(12):
            field[:, pl.ds(k * HALF + (13 * x + 12) * 8, 8), :] = jnp.zeros((2, 8, 128), F32)
    inputs[0].wait()

    def spread(x, carry):
        low = w_ref[x, :, 0:8, :]
        high = w_ref[x, :, 8:12, :]
        high = jnp.concatenate([high, high], axis=1)
        row = lax.broadcasted_iota(jnp.int32, (12, 8, 256), 1)
        upper = jnp.where(row < 2, pltpu.roll(low, 2, 1), jnp.where(row < 6, pltpu.roll(high, 2, 1), 0.0))
        base = pl.multiple_of(x * BLOCK, 8)
        for h in (0, 1):
            lanes = slice(128 * h, 128 * h + 128)
            field[h, pl.ds(base, 96), :] = low[:, :, lanes].reshape(96, 128)
            field[h, pl.ds(base + HALF, 96), :] = upper[:, :, lanes].reshape(96, 128)
        return carry

    lax.fori_loop(0, 12, spread, 0)
    for h in (0, 1):
        for at in range(len(DOWN)):
            pack_message(field, at, h, DOWN, groups[0][0])
    for copy in inputs[1:4]:
        copy.wait()

    ids = slots_ref[...]
    owner = ids >> 1
    d_x = (lax.axis_index("gx") - (owner >> 5)) & 7
    d_y = (lax.axis_index("gy") - ((owner >> 3) & 3)) & 3
    d_z = (lax.axis_index("gz") - (owner & 7)) & 7
    place = ((d_x * 2 + d_y) * 2 + d_z) * 2 + (ids & 1)
    place = jnp.where(ids < coupling_ref.shape[0], place, -1)
    order = jnp.broadcast_to(place, (16, 16)) == lax.broadcasted_iota(jnp.int32, (16, 16), 0)
    order = jnp.where(order, 1.0, 0.0).astype(BF16)
    p_high, p_low = exact_halves(p_ref[...])
    p_high = mm(order, p_high)
    p_low = mm(order, p_low)
    proj[:, pl.ds(1664, 256)] = jnp.zeros((48, 256), F32)
    proj[:, pl.ds(0, 1728)] = jnp.concatenate([p_high, p_low, p_high], axis=0)

    def picked(position, k, twice):
        plane = jnp.where(position >= BLOCK, 1, 0)
        inner = position - plane * BLOCK
        y, r = inner >> 3, inner & 7
        live = (y < 12) & ((r < 7) if k == 0 else ((r >= (0 if twice else 1)) & (r <= 5)))
        return jnp.where(live, 144 * plane + 12 * y + 6 * k + r, -1)

    picks = []
    for k in (0, 1):
        target = picked(lax.broadcasted_iota(jnp.int32, (PAIR, 1), 0), k, True)
        tall = lax.broadcasted_iota(jnp.int32, (PAIR, 384), 1) == target
        target = picked(lax.broadcasted_iota(jnp.int32, (1, PAIR), 1), k, False)
        wide = lax.broadcasted_iota(jnp.int32, (384, PAIR), 0) == target
        picks.append([jnp.where(v, 1.0, 0.0).astype(BF16) for v in (tall, wide)])
    for pair in range(6):
        begin = 288 * pair // 128 * 128
        window = proj[:, pl.ds(begin, 384)]
        if begin != 288 * pair:
            window = pltpu.roll(window, 384 - (288 * pair - begin), 1)
        window = window.astype(BF16)
        for k in (0, 1):
            proj_t[6 * k + pair] = mm_nt(picks[k][0], window).astype(BF16)
            proj_n[6 * k + pair] = mm(window[0:32], picks[k][1]).astype(BF16)

    def pair_rows(kp):
        return pl.ds((kp // 6) * HALF + (kp % 6) * PAIR, PAIR)

    def set_coefficients(values, app, h):
        total = jnp.zeros((16, 128), F32)
        for kp in range(12):
            high, low = exact_halves(values[h, pair_rows(kp), :])
            rows = proj_n[kp]
            both = mm(rows, high)
            total = total + (both[0:16] + (both[16:32] + mm(rows[0:16], low)))
        for g in range(8):
            nl_send[app, g, :, pl.ds(128 * h, 128)] = total[2 * g : 2 * g + 2]

    def start_coefficients(app):
        copies = []
        for at, bits in enumerate(BITS):
            copy = pltpu.make_async_remote_copy(
                src_ref=nl_send.at[app, at + 1],
                dst_ref=nl_recv.at[app, at + 1],
                send_sem=nl_sems.at[0, app, at],
                recv_sem=nl_sems.at[1, app, at],
                device_id=neighbour(tuple(-b for b in bits)),
                device_id_type=MESH,
            )
            copy.start()
            copies.append(copy)
        return copies

    def start_totals(app, copies):
        total = nl_send[app, 0]
        for at, copy in enumerate(copies):
            copy.wait_recv()
            total = total + nl_recv[app, at + 1]
        own = ((lax.axis_index("gx") * 4 + lax.axis_index("gy")) * 8 + lax.axis_index("gz")) * 2
        row = lax.broadcasted_iota(jnp.int32, (2, 256), 0)
        weight = jnp.where(row == 0, coupling_ref[own], coupling_ref[own + 1])
        nl_own[app] = total * weight
        out = []
        for at, bits in enumerate(BITS):
            copy = pltpu.make_async_remote_copy(
                src_ref=nl_own.at[app],
                dst_ref=nl_back.at[app, at + 1],
                send_sem=nl_sems.at[0, app, 7 + at],
                recv_sem=nl_sems.at[1, app, 7 + at],
                device_id=neighbour(bits),
                device_id_type=MESH,
            )
            copy.start()
            out.append(copy)
        return out

    def weighted_totals(app, copies):
        parts = [nl_own[app]]
        for at, copy in enumerate(copies):
            copy.wait_recv()
            parts.append(nl_back[app, at + 1])
        high, low = exact_halves(jnp.concatenate(parts, axis=0))
        return jnp.concatenate([high, high, low], axis=0)

    def add_nonlocal(total, h, back, k):
        for kp in range(6 * k, 6 * k + 6):
            rows = pair_rows(kp)
            total[h, rows, :] = total[h, rows, :] + mm(proj_t[kp], back[:, 128 * h : 128 * h + 128])

    def cells(values, total, h, k):
        for ij in range(4):
            i, j = ij // 2, ij % 2
            base = k * HALF + i * (6 * BLOCK) + j * 48
            rows = [pl.ds(base + a * BLOCK, 56) for a in range(7)]
            stacked = jnp.concatenate([values[h, r, :] for r in rows], axis=0).astype(BF16)
            product = mm(pad_k[2 * ij + k], stacked)
            for a in range(7):
                shared = 56 if i and a == 0 else 8 if j else 0
                if shared:
                    rows = pl.ds(base + a * BLOCK, shared)
                    total[h, rows, :] = total[h, rows, :] + product[56 * a : 56 * a + shared]
                if shared < 56:
                    rows = pl.ds(base + a * BLOCK + shared, 56 - shared)
                    total[h, rows, :] = product[56 * a + shared : 56 * a + 56]

    def join_middle(total, h):
        low, high = pl.ds(6, LINES, 8), pl.ds(HALF, LINES, 8)
        both = total[h, low, :] + total[h, high, :]
        total[h, low, :] = both
        total[h, high, :] = both

    for h in (0, 1):
        set_coefficients(field, 0, h)

    pl.semaphore_wait(barrier, len(ALL))
    reduce_1 = start_coefficients(0)
    waits = [*reduce_1]
    first = []
    for h in (0, 1):
        first.append({at: exchange_copy(at, h, DOWN, groups[0]) for at in range(len(DOWN))})
        for at in [*chosen_of(DOWN, lambda d: d[2] < 0), *chosen_of(DOWN, lambda d: d[2] == 0)]:
            first[h][at].start()
        waits += first[h].values()

    col = lax.broadcasted_iota(jnp.int32, (343, PAD_NODES), 1)
    node = jnp.where((col & 7) < 7, (col >> 3) * 7 + (col & 7), -1)
    widen = jnp.where(lax.broadcasted_iota(jnp.int32, (343, PAD_NODES), 0) == node, 1.0, 0.0).astype(BF16)
    inputs[4].wait()

    loose[:, pl.ds(680, 24), :] = jnp.zeros((4, 24, 128), F32)

    def pad_cells(ij, carry):
        wide = mm(k_ref[ij].reshape(686, 343), widen)
        for t in range(4):
            width = min(128, PAD_NODES - 128 * t)
            loose[t, pl.ds(0, 686), pl.ds(0, width)] = wide[:, 128 * t : 128 * t + width]
        for t in range(4):
            width = min(128, PAD_NODES - 128 * t)
            for k in (0, 1):
                runs = [loose[t, pl.ds(14 * run + k, 8, 2), :] for run in range(49)]
                tall = jnp.concatenate(runs, axis=0).astype(BF16)
                pad_k[2 * ij + k, :, pl.ds(128 * t, width)] = tall[:, 0:width]
        return carry

    lax.fori_loop(0, 3, pad_cells, 0)
    totals_1 = start_totals(0, reduce_1)
    waits += totals_1
    lax.fori_loop(3, 4, pad_cells, 0)

    above = chosen_of(ALL, lambda d: d[2] > 0)
    beside = chosen_of(ALL, lambda d: d[2] <= 0 and max(d) > 0)
    below = [at for at in range(len(ALL)) if at not in above and at not in beside]
    owned = chosen_of(ALL, lambda d: min(d) >= 0)
    other = [at for at in range(len(ALL)) if at not in owned]
    everything = range(len(DOWN))
    middle = []
    for h in (0, 1):
        end_exchange(field, h, chosen_of(DOWN, lambda d: d[2] == 0), DOWN, first[h], groups[0][1], False)
        cells(field, image, h, 0)
    for h in (0, 1):
        end_exchange(field, h, chosen_of(DOWN, lambda d: d[2] < 0), DOWN, first[h], groups[0][1], False)
        cells(field, image, h, 1)
        copies = start_exchange(image, h, above, ALL, groups[1])
        join_middle(image, h)
        copies.update(start_exchange(image, h, beside, ALL, groups[1]))
        middle.append(copies)
    back = weighted_totals(0, totals_1)
    for h in (0, 1):
        add_nonlocal(image, h, back, 0)
        middle[h].update(start_exchange(image, h, [at for at in below if ALL[at][2] < 0], ALL, groups[1]))
        add_nonlocal(image, h, back, 1)
        middle[h].update(start_exchange(image, h, [at for at in below if ALL[at][2] == 0], ALL, groups[1]))
        waits += middle[h].values()

    last = []
    for h in (0, 1):
        end_exchange(image, h, owned, ALL, middle[h], groups[1][1], True)
        set_coefficients(image, 1, h)
    reduce_2 = start_coefficients(1)
    waits += reduce_2
    for h in (0, 1):
        end_exchange(image, h, [at for at in other if ALL[at][2] >= 0], ALL, middle[h], groups[1][1], True)
        cells(image, field, h, 0)
        if h == 1:
            totals_2 = start_totals(1, reduce_2)
            waits += totals_2
        end_exchange(image, h, [at for at in other if ALL[at][2] < 0], ALL, middle[h], groups[1][1], True)
        cells(image, field, h, 1)
        copies = start_exchange(field, h, chosen_of(UP, lambda d: d[2] > 0), UP, groups[2])
        join_middle(field, h)
        copies.update(start_exchange(field, h, chosen_of(UP, lambda d: d[2] == 0), UP, groups[2]))
        last.append(copies)
        waits += copies.values()
    back = None
    for h in (0, 1):
        end_exchange(field, h, everything, UP, last[h], groups[2][1], True)
        if back is None:
            back = weighted_totals(1, totals_2)
        lanes = slice(128 * h, 128 * h + 128)

        def finish(pair, carry):
            base = pl.multiple_of(pair * PAIR, 8)
            total = []
            for k in (0, 1):
                total.append(field[h, pl.ds(base + k * HALF, PAIR), :] + mm(proj_t[6 * k + pair], back[:, lanes]))
            row = lax.broadcasted_iota(jnp.int32, (12, 8, 128), 1)
            for plane in (0, 1):
                x = 2 * pair + plane
                at = plane * BLOCK
                low = total[0][at : at + 96].reshape(12, 8, 128)
                high = pltpu.roll(total[1][at : at + 96].reshape(12, 8, 128), 6, 1)
                out_ref[x, :, 0:8, lanes] = 2.0 * jnp.where(row < 7, low, high) - w_ref[x, :, 0:8, lanes]
                out_ref[x, :, 8:12, lanes] = 2.0 * high[:, 0:4] - w_ref[x, :, 8:12, lanes]
            return carry

        lax.fori_loop(0, 6, finish, 0)
    for copy in waits:
        copy.wait_send()


def local(wavefunctions, cell_matrices, projectors, slot_atoms, atom_coupling):
    buffers = []
    for deltas in (DOWN, ALL, UP):
        one = [
            pltpu.VMEM((2, tiled(message_rows(kind_of(d), deltas is ALL)), 128), message_type(kind_of(d)))
            for d in deltas
        ]
        buffers += one + one
    count = len(DOWN) + len(ALL) + len(UP)
    vmem = pl.BlockSpec(memory_space=pltpu.VMEM)
    return pl.pallas_call(
        kernel,
        out_shape=jax.ShapeDtypeStruct(wavefunctions.shape, F32),
        in_specs=[pl.BlockSpec(memory_space=pltpu.HBM)] * 5,
        out_specs=vmem,
        scratch_shapes=[
            pltpu.VMEM((12, 12, 12, 256), F32),
            pltpu.VMEM((4, 343, 2, 343), BF16),
            pltpu.VMEM((16, 1728), F32),
            pltpu.VMEM((1, 16), jnp.int32),
            pltpu.SMEM((512,), F32),
            pltpu.SemaphoreType.DMA((5,)),
            pltpu.VMEM((2, ROWS, 128), F32),
            pltpu.VMEM((2, ROWS, 128), F32),
            pltpu.VMEM((8, PAD_NODES, PAD_NODES), BF16),
            pltpu.VMEM((48, 1920), F32),
            pltpu.VMEM((12, 32, PAIR), BF16),
            pltpu.VMEM((12, PAIR, 48), BF16),
            pltpu.VMEM((2, 8, 2, 256), F32),
            pltpu.VMEM((2, 8, 2, 256), F32),
            pltpu.VMEM((2, 2, 256), F32),
            pltpu.VMEM((2, 8, 2, 256), F32),
            pltpu.SemaphoreType.DMA((2, 2, 14)),
            pltpu.SemaphoreType.DMA((2, count, 2)),
            *buffers,
            pltpu.VMEM((4, 704, 128), F32),
        ],
        compiler_params=pltpu.CompilerParams(collective_id=0, has_side_effects=True, vmem_limit_bytes=40 * 1024 * 1024),
    )(
        *(
            pltpu.with_memory_space_constraint(array, pltpu.HBM)
            for array in (
                wavefunctions,
                cell_matrices.transpose(0, 1, 3, 2, 4).reshape(4, 343, 2, 343),
                projectors[0],
                slot_atoms,
                atom_coupling,
            )
        )
    )


def solution(mesh):
    return jax.shard_map(
        local,
        mesh=mesh,
        in_specs=(
            P("gx", "gy", "gz", None),
            P("gx", "gy", "gz", None, None),
            P(("gx", "gy", "gz"), None, None),
            P(("gx", "gy", "gz"), None),
            P(),
        ),
        out_specs=P("gx", "gy", "gz", None),
        check_vma=False,
    )
```

```python
import itertools

import jax
import jax.numpy as jnp
from jax import lax
from jax.experimental import pallas as pl
from jax.experimental.pallas import tpu as pltpu
from jax.sharding import PartitionSpec as P

MESH = pl.DeviceIdType.MESH
F32 = jnp.float32
BF16 = jnp.bfloat16

LINES = 169
HALF = LINES * 8
ROWS = 2 * HALF
BLOCK = 104
PAIR = 2 * BLOCK
PAD_NODES = 392

ALL = [d for d in itertools.product((-1, 0, 1), repeat=3) if any(d)]
ALL.sort(key=lambda d: (sum(map(abs, d)), -abs(d[2])))
DOWN = [d for d in ALL if max(d) <= 0]
UP = [d for d in ALL if min(d) >= 0]
BITS = [d for d in itertools.product((0, 1), repeat=3) if any(d)]


def kind_of(delta):
    return tuple(int(d != 0) for d in delta)


def message_rows(kind, full):
    return {
        (1, 0, 0): 208,
        (0, 1, 0): LINES if full else 156,
        (0, 0, 1): LINES if full else 156,
        (1, 1, 0): 16,
        (1, 0, 1): 13,
        (0, 1, 1): 13,
        (1, 1, 1): 1,
    }[kind]


def tiled(rows):
    return -(-rows // 16) * 16 if rows > 1 else 1


def message_type(kind):
    return F32 if kind == (1, 1, 1) else BF16


def z_row(z):
    return 0 if z == 0 else HALF + 6


def pieces_of(kind, coords, full):
    x, y, z = coords
    if kind == (1, 0, 0):
        return [(k * HALF + x * BLOCK, BLOCK, 1) for k in (0, 1)]
    if kind == (0, 1, 0):
        nodes = [*range(7), *range(HALF + 1, HALF + 7)]
        return [(row + y * 8, 13 if full else 12, BLOCK) for row in nodes]
    if kind == (0, 0, 1):
        return [(z_row(z), LINES if full else 156, 8)]
    if kind == (1, 1, 0):
        return [(k * HALF + (13 * x + y) * 8, 8, 1) for k in (0, 1)]
    if kind == (1, 0, 1):
        return [(z_row(z) + x * BLOCK, 13, 8)]
    if kind == (0, 1, 1):
        return [(z_row(z) + y * 8, 13, BLOCK)]
    return [(z_row(z) + (13 * x + y) * 8, 1, 1)]


def rows_at(start, count, stride):
    return pl.ds(start, count) if stride == 1 else pl.ds(start, count, stride)


def packed(field, h, kind, coords, full):
    parts = [field[h, rows_at(*p), :] for p in pieces_of(kind, coords, full)]
    return parts[0] if len(parts) == 1 else jnp.concatenate(parts, axis=0)


def merge(field, h, kind, coords, full, message, adding):
    at = 0
    for start, count, stride in pieces_of(kind, coords, full):
        part = message[at : at + count]
        rows = rows_at(start, count, stride)
        value = field[h, rows, :] + part if adding else part
        field[h, rows, :] = value
        if kind == (0, 1, 0) and start == 6 + 8 * coords[1]:
            field[h, rows_at(start - 6 + HALF, count, stride), :] = value
        at += count


def both_halves(field, rows):
    return jnp.concatenate([field[0, rows, :], field[1, rows, :]], axis=1)


def neighbour(delta):
    out = []
    for name, d in zip(("gx", "gy", "gz"), delta):
        size = lax.axis_size(name)
        out.append((lax.axis_index(name) + d + size) % size)
    return tuple(out)


def exchange_copy(at, h, deltas, group):
    send, recv, send_sem, recv_sem = group
    return pltpu.make_async_remote_copy(
        src_ref=send[at].at[h],
        dst_ref=recv[at].at[h],
        send_sem=send_sem.at[at, h],
        recv_sem=recv_sem.at[at, h],
        device_id=neighbour(deltas[at]),
        device_id_type=MESH,
    )


def pack_message(field, at, h, deltas, send):
    kind = kind_of(deltas[at])
    coords = tuple(12 if d > 0 else 0 for d in deltas[at])
    value = packed(field, h, kind, coords, deltas is ALL).astype(message_type(kind))
    send[at][h, pl.ds(0, value.shape[0]), :] = value


def start_exchange(field, h, chosen, deltas, group):
    copies = {}
    for at in chosen:
        pack_message(field, at, h, deltas, group[0])
        copies[at] = exchange_copy(at, h, deltas, group)
        copies[at].start()
    return copies


def end_exchange(field, h, chosen, deltas, copies, recv, adding):
    for at in sorted(chosen, key=lambda at: abs(deltas[at][2])):
        copies[at].wait_recv()
        coords = tuple(12 if d < 0 else 0 for d in deltas[at])
        full = deltas is ALL
        message = recv[at][h, pl.ds(0, message_rows(kind_of(deltas[at]), full)), :].astype(F32)
        merge(field, h, kind_of(deltas[at]), coords, full, message, adding)


def chosen_of(deltas, test):
    return [at for at, d in enumerate(deltas) if test(d)]


def exact_halves(values):
    high = values.astype(BF16)
    return high, (values - high.astype(F32)).astype(BF16)


def mm(a, b):
    return jnp.dot(a, b, preferred_element_type=F32)


def mm_nt(a, b):
    return lax.dot_general(a, b, (((1,), (1,)), ((), ())), preferred_element_type=F32)


def kernel(w_hbm, k_hbm, p_hbm, slots_hbm, coupling_hbm, out_ref, *scratch):
    w_ref, k_ref, p_ref, slots_ref, coupling_ref, in_sems = scratch[:6]
    scratch = scratch[6:]
    (field, image, pad_k, proj, proj_n, proj_t) = scratch[:6]
    loose, scratch = scratch[-1], scratch[:-1]
    nl_send, nl_recv, nl_own, nl_back, nl_sems = scratch[6:11]
    sems = scratch[11]
    buffers = scratch[12:]
    at = 0
    groups = []
    sem_at = 0
    for deltas in (DOWN, ALL, UP):
        n = len(deltas)
        groups.append(
            (
                buffers[at : at + n],
                buffers[at + n : at + 2 * n],
                sems.at[0, pl.ds(sem_at, n)],
                sems.at[1, pl.ds(sem_at, n)],
            )
        )
        at += 2 * n
        sem_at += n

    inputs = [
        pltpu.make_async_copy(source, target, in_sems.at[at])
        for at, (source, target) in enumerate(
            (
                (w_hbm, w_ref),
                (slots_hbm, slots_ref),
                (p_hbm, p_ref),
                (coupling_hbm, coupling_ref),
                (k_hbm, k_ref),
            )
        )
    ]
    for copy in inputs:
        copy.start()

    barrier = pltpu.get_barrier_semaphore()
    for delta in reversed(ALL):
        pl.semaphore_signal(barrier, inc=1, device_id=neighbour(delta), device_id_type=MESH)

    for k in (0, 1):
        for x in range(12):
            field[:, pl.ds(k * HALF + (13 * x + 12) * 8, 8), :] = jnp.zeros((2, 8, 128), F32)
    inputs[0].wait()

    def spread(x, carry):
        low = w_ref[x, :, 0:8, :]
        high = w_ref[x, :, 8:12, :]
        high = jnp.concatenate([high, high], axis=1)
        row = lax.broadcasted_iota(jnp.int32, (12, 8, 256), 1)
        upper = jnp.where(row < 2, pltpu.roll(low, 2, 1), jnp.where(row < 6, pltpu.roll(high, 2, 1), 0.0))
        base = pl.multiple_of(x * BLOCK, 8)
        for h in (0, 1):
            lanes = slice(128 * h, 128 * h + 128)
            field[h, pl.ds(base, 96), :] = low[:, :, lanes].reshape(96, 128)
            field[h, pl.ds(base + HALF, 96), :] = upper[:, :, lanes].reshape(96, 128)
        return carry

    lax.fori_loop(0, 12, spread, 0)
    for h in (0, 1):
        for at in range(len(DOWN)):
            pack_message(field, at, h, DOWN, groups[0][0])
    for copy in inputs[1:4]:
        copy.wait()

    ids = slots_ref[...]
    owner = ids >> 1
    d_x = (lax.axis_index("gx") - (owner >> 5)) & 7
    d_y = (lax.axis_index("gy") - ((owner >> 3) & 3)) & 3
    d_z = (lax.axis_index("gz") - (owner & 7)) & 7
    place = ((d_x * 2 + d_y) * 2 + d_z) * 2 + (ids & 1)
    place = jnp.where(ids < coupling_ref.shape[0], place, -1)
    order = jnp.broadcast_to(place, (16, 16)) == lax.broadcasted_iota(jnp.int32, (16, 16), 0)
    order = jnp.where(order, 1.0, 0.0).astype(BF16)
    p_high, p_low = exact_halves(p_ref[...])
    p_high = mm(order, p_high)
    p_low = mm(order, p_low)
    proj[:, pl.ds(1664, 256)] = jnp.zeros((48, 256), F32)
    proj[:, pl.ds(0, 1728)] = jnp.concatenate([p_high, p_low, p_high], axis=0)

    def picked(position, k, twice):
        plane = jnp.where(position >= BLOCK, 1, 0)
        inner = position - plane * BLOCK
        y, r = inner >> 3, inner & 7
        live = (y < 12) & ((r < 7) if k == 0 else ((r >= (0 if twice else 1)) & (r <= 5)))
        return jnp.where(live, 144 * plane + 12 * y + 6 * k + r, -1)

    picks = []
    for k in (0, 1):
        target = picked(lax.broadcasted_iota(jnp.int32, (PAIR, 1), 0), k, True)
        tall = lax.broadcasted_iota(jnp.int32, (PAIR, 384), 1) == target
        target = picked(lax.broadcasted_iota(jnp.int32, (1, PAIR), 1), k, False)
        wide = lax.broadcasted_iota(jnp.int32, (384, PAIR), 0) == target
        picks.append([jnp.where(v, 1.0, 0.0).astype(BF16) for v in (tall, wide)])
    for pair in range(6):
        begin = 288 * pair // 128 * 128
        window = proj[:, pl.ds(begin, 384)]
        if begin != 288 * pair:
            window = pltpu.roll(window, 384 - (288 * pair - begin), 1)
        window = window.astype(BF16)
        for k in (0, 1):
            proj_t[6 * k + pair] = mm_nt(picks[k][0], window).astype(BF16)
            proj_n[6 * k + pair] = mm(window[0:32], picks[k][1]).astype(BF16)

    def pair_rows(kp):
        return pl.ds((kp // 6) * HALF + (kp % 6) * PAIR, PAIR)

    def set_coefficients(values, app, h):
        total = jnp.zeros((16, 128), F32)
        for kp in range(12):
            high, low = exact_halves(values[h, pair_rows(kp), :])
            rows = proj_n[kp]
            both = mm(rows, high)
            total = total + (both[0:16] + (both[16:32] + mm(rows[0:16], low)))
        for g in range(8):
            nl_send[app, g, :, pl.ds(128 * h, 128)] = total[2 * g : 2 * g + 2]

    def start_coefficients(app):
        copies = []
        for at, bits in enumerate(BITS):
            copy = pltpu.make_async_remote_copy(
                src_ref=nl_send.at[app, at + 1],
                dst_ref=nl_recv.at[app, at + 1],
                send_sem=nl_sems.at[0, app, at],
                recv_sem=nl_sems.at[1, app, at],
                device_id=neighbour(tuple(-b for b in bits)),
                device_id_type=MESH,
            )
            copy.start()
            copies.append(copy)
        return copies

    def start_totals(app, copies):
        total = nl_send[app, 0]
        for at, copy in enumerate(copies):
            copy.wait_recv()
            total = total + nl_recv[app, at + 1]
        own = ((lax.axis_index("gx") * 4 + lax.axis_index("gy")) * 8 + lax.axis_index("gz")) * 2
        row = lax.broadcasted_iota(jnp.int32, (2, 256), 0)
        weight = jnp.where(row == 0, coupling_ref[own], coupling_ref[own + 1])
        nl_own[app] = total * weight
        out = []
        for at, bits in enumerate(BITS):
            copy = pltpu.make_async_remote_copy(
                src_ref=nl_own.at[app],
                dst_ref=nl_back.at[app, at + 1],
                send_sem=nl_sems.at[0, app, 7 + at],
                recv_sem=nl_sems.at[1, app, 7 + at],
                device_id=neighbour(bits),
                device_id_type=MESH,
            )
            copy.start()
            out.append(copy)
        return out

    def weighted_totals(app, copies):
        parts = [nl_own[app]]
        for at, copy in enumerate(copies):
            copy.wait_recv()
            parts.append(nl_back[app, at + 1])
        high, low = exact_halves(jnp.concatenate(parts, axis=0))
        return jnp.concatenate([high, high, low], axis=0)

    def add_nonlocal(total, h, back, k):
        for kp in range(6 * k, 6 * k + 6):
            rows = pair_rows(kp)
            total[h, rows, :] = total[h, rows, :] + mm(proj_t[kp], back[:, 128 * h : 128 * h + 128])

    def cells(values, total, h, k):
        for ij in range(4):
            i, j = ij // 2, ij % 2
            base = k * HALF + i * (6 * BLOCK) + j * 48
            rows = [pl.ds(base + a * BLOCK, 56) for a in range(7)]
            stacked = jnp.concatenate([values[h, r, :] for r in rows], axis=0).astype(BF16)
            product = mm(pad_k[2 * ij + k], stacked)
            for a in range(7):
                shared = 56 if i and a == 0 else 8 if j else 0
                if shared:
                    rows = pl.ds(base + a * BLOCK, shared)
                    total[h, rows, :] = total[h, rows, :] + product[56 * a : 56 * a + shared]
                if shared < 56:
                    rows = pl.ds(base + a * BLOCK + shared, 56 - shared)
                    total[h, rows, :] = product[56 * a + shared : 56 * a + 56]

    def join_middle(total, h):
        low, high = pl.ds(6, LINES, 8), pl.ds(HALF, LINES, 8)
        both = total[h, low, :] + total[h, high, :]
        total[h, low, :] = both
        total[h, high, :] = both

    for h in (0, 1):
        set_coefficients(field, 0, h)

    pl.semaphore_wait(barrier, len(ALL))
    reduce_1 = start_coefficients(0)
    waits = [*reduce_1]
    first = []
    for h in (0, 1):
        first.append({at: exchange_copy(at, h, DOWN, groups[0]) for at in range(len(DOWN))})
        for at in [*chosen_of(DOWN, lambda d: d[2] < 0), *chosen_of(DOWN, lambda d: d[2] == 0)]:
            first[h][at].start()
        waits += first[h].values()

    col = lax.broadcasted_iota(jnp.int32, (343, PAD_NODES), 1)
    node = jnp.where((col & 7) < 7, (col >> 3) * 7 + (col & 7), -1)
    widen = jnp.where(lax.broadcasted_iota(jnp.int32, (343, PAD_NODES), 0) == node, 1.0, 0.0).astype(BF16)
    inputs[4].wait()

    loose[:, pl.ds(680, 24), :] = jnp.zeros((4, 24, 128), F32)

    def pad_cells(ij, carry):
        wide = mm(k_ref[ij].reshape(686, 343), widen)
        for t in range(4):
            width = min(128, PAD_NODES - 128 * t)
            loose[t, pl.ds(0, 686), pl.ds(0, width)] = wide[:, 128 * t : 128 * t + width]
        for t in range(4):
            width = min(128, PAD_NODES - 128 * t)
            for k in (0, 1):
                runs = [loose[t, pl.ds(14 * run + k, 8, 2), :] for run in range(49)]
                tall = jnp.concatenate(runs, axis=0).astype(BF16)
                pad_k[2 * ij + k, :, pl.ds(128 * t, width)] = tall[:, 0:width]
        return carry

    lax.fori_loop(0, 3, pad_cells, 0)
    totals_1 = start_totals(0, reduce_1)
    waits += totals_1
    lax.fori_loop(3, 4, pad_cells, 0)

    above = chosen_of(ALL, lambda d: d[2] > 0)
    beside = chosen_of(ALL, lambda d: d[2] <= 0 and max(d) > 0)
    below = [at for at in range(len(ALL)) if at not in above and at not in beside]
    owned = chosen_of(ALL, lambda d: min(d) >= 0)
    other = [at for at in range(len(ALL)) if at not in owned]
    everything = range(len(DOWN))
    middle = []
    for h in (0, 1):
        end_exchange(field, h, chosen_of(DOWN, lambda d: d[2] == 0), DOWN, first[h], groups[0][1], False)
        cells(field, image, h, 0)
    for h in (0, 1):
        end_exchange(field, h, chosen_of(DOWN, lambda d: d[2] < 0), DOWN, first[h], groups[0][1], False)
        cells(field, image, h, 1)
        copies = start_exchange(image, h, above, ALL, groups[1])
        join_middle(image, h)
        copies.update(start_exchange(image, h, beside, ALL, groups[1]))
        middle.append(copies)
    back = weighted_totals(0, totals_1)
    for h in (0, 1):
        add_nonlocal(image, h, back, 0)
        middle[h].update(start_exchange(image, h, [at for at in below if ALL[at][2] < 0], ALL, groups[1]))
        add_nonlocal(image, h, back, 1)
        middle[h].update(start_exchange(image, h, [at for at in below if ALL[at][2] == 0], ALL, groups[1]))
        waits += middle[h].values()

    last = []
    for h in (0, 1):
        end_exchange(image, h, owned, ALL, middle[h], groups[1][1], True)
        set_coefficients(image, 1, h)
    reduce_2 = start_coefficients(1)
    waits += reduce_2
    for h in (0, 1):
        end_exchange(image, h, [at for at in other if ALL[at][2] >= 0], ALL, middle[h], groups[1][1], True)
        cells(image, field, h, 0)
        end_exchange(image, h, [at for at in other if ALL[at][2] < 0], ALL, middle[h], groups[1][1], True)
        if h == 0:
            totals_2 = start_totals(1, reduce_2)
            waits += totals_2
        cells(image, field, h, 1)
        copies = start_exchange(field, h, chosen_of(UP, lambda d: d[2] > 0), UP, groups[2])
        join_middle(field, h)
        copies.update(start_exchange(field, h, chosen_of(UP, lambda d: d[2] == 0), UP, groups[2]))
        last.append(copies)
        waits += copies.values()
    back = None
    for h in (0, 1):
        end_exchange(field, h, everything, UP, last[h], groups[2][1], True)
        if back is None:
            back = weighted_totals(1, totals_2)
        lanes = slice(128 * h, 128 * h + 128)

        def finish(pair, carry):
            base = pl.multiple_of(pair * PAIR, 8)
            total = []
            for k in (0, 1):
                total.append(field[h, pl.ds(base + k * HALF, PAIR), :] + mm(proj_t[6 * k + pair], back[:, lanes]))
            row = lax.broadcasted_iota(jnp.int32, (12, 8, 128), 1)
            for plane in (0, 1):
                x = 2 * pair + plane
                at = plane * BLOCK
                low = total[0][at : at + 96].reshape(12, 8, 128)
                high = pltpu.roll(total[1][at : at + 96].reshape(12, 8, 128), 6, 1)
                out_ref[x, :, 0:8, lanes] = 2.0 * jnp.where(row < 7, low, high) - w_ref[x, :, 0:8, lanes]
                out_ref[x, :, 8:12, lanes] = 2.0 * high[:, 0:4] - w_ref[x, :, 8:12, lanes]
            return carry

        lax.fori_loop(0, 6, finish, 0)
    for copy in waits:
        copy.wait_send()


def local(wavefunctions, cell_matrices, projectors, slot_atoms, atom_coupling):
    buffers = []
    for deltas in (DOWN, ALL, UP):
        one = [
            pltpu.VMEM((2, tiled(message_rows(kind_of(d), deltas is ALL)), 128), message_type(kind_of(d)))
            for d in deltas
        ]
        buffers += one + one
    count = len(DOWN) + len(ALL) + len(UP)
    vmem = pl.BlockSpec(memory_space=pltpu.VMEM)
    return pl.pallas_call(
        kernel,
        out_shape=jax.ShapeDtypeStruct(wavefunctions.shape, F32),
        in_specs=[pl.BlockSpec(memory_space=pltpu.HBM)] * 5,
        out_specs=vmem,
        scratch_shapes=[
            pltpu.VMEM((12, 12, 12, 256), F32),
            pltpu.VMEM((4, 343, 2, 343), BF16),
            pltpu.VMEM((16, 1728), F32),
            pltpu.VMEM((1, 16), jnp.int32),
            pltpu.SMEM((512,), F32),
            pltpu.SemaphoreType.DMA((5,)),
            pltpu.VMEM((2, ROWS, 128), F32),
            pltpu.VMEM((2, ROWS, 128), F32),
            pltpu.VMEM((8, PAD_NODES, PAD_NODES), BF16),
            pltpu.VMEM((48, 1920), F32),
            pltpu.VMEM((12, 32, PAIR), BF16),
            pltpu.VMEM((12, PAIR, 48), BF16),
            pltpu.VMEM((2, 8, 2, 256), F32),
            pltpu.VMEM((2, 8, 2, 256), F32),
            pltpu.VMEM((2, 2, 256), F32),
            pltpu.VMEM((2, 8, 2, 256), F32),
            pltpu.SemaphoreType.DMA((2, 2, 14)),
            pltpu.SemaphoreType.DMA((2, count, 2)),
            *buffers,
            pltpu.VMEM((4, 704, 128), F32),
        ],
        compiler_params=pltpu.CompilerParams(collective_id=0, has_side_effects=True, vmem_limit_bytes=40 * 1024 * 1024),
    )(
        *(
            pltpu.with_memory_space_constraint(array, pltpu.HBM)
            for array in (
                wavefunctions,
                cell_matrices.transpose(0, 1, 3, 2, 4).reshape(4, 343, 2, 343),
                projectors[0],
                slot_atoms,
                atom_coupling,
            )
        )
    )


def solution(mesh):
    return jax.shard_map(
        local,
        mesh=mesh,
        in_specs=(
            P("gx", "gy", "gz", None),
            P("gx", "gy", "gz", None, None),
            P(("gx", "gy", "gz"), None, None),
            P(("gx", "gy", "gz"), None),
            P(),
        ),
        out_specs=P("gx", "gy", "gz", None),
        check_vma=False,
    )
```
